32 devices in a mesh: tm: 4 (over z), space: 8 (over y, x, core).
Axes of the slice: x: 2, y: 2, z: 4, core: 2. Of those that a mesh axis runs over, the one named last changes fastest.
Arguments:
- frames: bfloat16 [4, 96, 32, 1280], P('tm', None, 'space'), may hold values from -6 to 6
- cache: bfloat16 [2, 96, 32, 1280], P(None, 'tm', 'space'), may hold values from -6 to 6
- grad_out: bfloat16 [4, 96, 32, 1280], P('tm', None, 'space'), may hold values from -6 to 6
- weight: bfloat16 [3, 3, 3, 96, 96], replicated, may hold values from -0.125 to 0.125
Outputs:
- input_grad: bfloat16 [4, 96, 32, 1280], P('tm', None, 'space')
- cache_grad: bfloat16 [2, 96, 32, 1280], P(None, 'tm', 'space')
- weight_grad: float32 [3, 3, 3, 96, 96], replicated
The draws below stay inside these ranges and needn't reach their ends.
All inputs are finite; a program needn't handle non-finite values.
Results may differ from the reference program's by a relative error of at most 0.0041.
Values may be sent and summed in bfloat16 or wider, within the bound.
A program may use at most 64 MiB of HBM per device.

```python
import math
import jax
import jax.numpy as jnp
from jax import lax

C = 96
WIDTH = 1280
FRAMES = 4
HEIGHT = 32


def level_of(key, dims, shards, least, largest):
    loudness = 1.0
    for dim, blocks in shards:
        steps = jax.random.uniform(jax.random.fold_in(jax.random.fold_in(key, 6), dim), (blocks,), jnp.float32, least / len(shards), largest / len(shards))
        loudness = loudness * jnp.repeat(jnp.exp(steps), dims[dim] // blocks).reshape((-1,) + (1,) * (len(dims) - 1 - dim))
    return loudness


def centred(own_key, dims, spread, most, cuts=(), kind=jnp.bfloat16):
    array = jax.random.normal(own_key, dims, jnp.float32) * spread
    if len(cuts) > 0:
        array = level_of(own_key, dims, cuts, -0.22, 0.18) * array
    return jnp.clip(array, min=-most, max=most).astype(kind)


def setup_inputs(seed: int = 0) -> dict:
    key_of = jax.random.split(jax.random.key(seed), 5)
    return {
        "frames": centred(key_of[0], (FRAMES, C, HEIGHT, WIDTH), 1.0, 6.0, ((0, 4), (2, 8))),
        "cache": centred(key_of[1], (2, C, HEIGHT, WIDTH), 1.0, 6.0, ((1, 4), (2, 8))),
        "grad_out": centred(key_of[2], (FRAMES, C, HEIGHT, WIDTH), 1.0, 6.0, ((0, 4), (2, 8))),
        "weight": centred(key_of[3], (3, 3, 3, C, C), (27 * C) ** -0.5, 0.125),
    }


def rounded(value):
    return lax.optimization_barrier(value.astype(jnp.bfloat16)).astype(jnp.float32)

def reference(frames, cache, grad_out, weight):
    extended = jnp.concatenate([cache, frames], axis=0)
    padded_in = jnp.pad(extended, ((0, 0), (0, 0), (1, 1), (1, 1)))
    padded_out = jnp.pad(grad_out, ((0, 0), (0, 0), (1, 1), (1, 1)))
    weight_full = weight.astype(jnp.float32)
    band = math.gcd(HEIGHT, 16)
    band_count = HEIGHT // band

    def one_band(band_index):
        start = (band_index * band).astype(jnp.int32)
        band_in = lax.dynamic_slice_in_dim(padded_in, start, band + 2, 2)
        band_out = lax.dynamic_slice_in_dim(padded_out, start, band + 2, 2)
        weight_sum = jnp.zeros((3, 3, 3, C, C), jnp.float32)
        terms = []
        for frame_index in range(FRAMES):
            accum = jnp.zeros((3, C, band, WIDTH), jnp.float32)
            grad_full = band_out[frame_index, :, 1:1 + band, 1:1 + WIDTH].astype(jnp.float32)
            for row_tap in range(3):
                for col_tap in range(3):
                    window = band_out[frame_index, :, 2 - row_tap:2 - row_tap + band, 2 - col_tap:2 - col_tap + WIDTH].astype(jnp.float32)
                    accum = accum + jnp.einsum('koc,ohw->kchw', weight_full[:, row_tap, col_tap], window, precision=lax.Precision.HIGHEST)
                    inputs = band_in[frame_index:frame_index + 3, :, row_tap:row_tap + band, col_tap:col_tap + WIDTH].astype(jnp.float32)
                    contrib = jnp.einsum('ohw,kchw->koc', grad_full, inputs, precision=lax.Precision.HIGHEST)
                    weight_sum = weight_sum.at[:, row_tap, col_tap].add(contrib)
            terms.append(accum)
        grads = []
        for frame_index in range(FRAMES):
            total = terms[frame_index][2]
            if frame_index + 1 < FRAMES:
                total = total + rounded(terms[frame_index + 1][1])
            if frame_index + 2 < FRAMES:
                total = total + rounded(terms[frame_index + 2][0])
            grads.append(total.astype(jnp.bfloat16))
        input_band = jnp.stack(grads, axis=0)
        cache_first = terms[0][0]
        cache_second = terms[0][1] + rounded(terms[1][0])
        cache_band = jnp.stack([cache_first, cache_second], axis=0).astype(jnp.bfloat16)
        return (input_band, cache_band, weight_sum)
    input_bands, cache_bands, weight_parts = lax.map(one_band, jnp.arange(band_count, dtype=jnp.int32))
    input_grad = jnp.transpose(input_bands, (1, 2, 0, 3, 4)).reshape(FRAMES, C, HEIGHT, WIDTH)
    cache_grad = jnp.transpose(cache_bands, (1, 2, 0, 3, 4)).reshape(2, C, HEIGHT, WIDTH)
    scale = 1.0 / math.sqrt(FRAMES * HEIGHT * WIDTH)
    weight_grad = lax.optimization_barrier(jnp.sum(weight_parts, axis=0)) * scale
    return (input_grad, cache_grad, weight_grad)
```

```python
import functools
import math

import jax
import jax.numpy as jnp
from jax import lax
from jax.experimental import pallas as pl
from jax.experimental.pallas import tpu as pltpu
from jax.sharding import PartitionSpec as P

MESH = pl.DeviceIdType.MESH
OWN, N1, N2, C1, C0 = range(5)
TO_PREV, FWD_PREV, TO_NEXT, FWD_C1, FWD_C0 = range(5)


def kernel(
    nz, ns, ck, channels, share, scale,
    g_hbm, x_hbm, c_hbm, w_hbm, ig_ref, cg_ref, wg_ref,
    g_ref, x_ref, c_ref, w_ref, wf,
    gp, sc, dacc, wtmp, acc, xs_ref, wl_ref,
    sb, rb, zs, zb, gb,
    loads, z_send, z_recv, h_send, h_recv,
    rs_send, rs_recv, zz_send, zz_recv, ag_send, ag_recv,
):
    assert nz == 4
    j = lax.axis_index("tm")
    s = lax.axis_index("space")
    _, rows, cols = g_ref.shape
    k_row = 3 * channels
    taps = 3 * k_row
    last = nz - 1
    order = [0, rows - 1, *range(1, rows - 1)]
    high = 128
    late = jnp.where(j < last - 1, N2, C1)

    fetch = [
        pltpu.make_async_copy(src, dst, loads.at[n])
        for n, (src, dst) in enumerate(((g_hbm, g_ref), (w_hbm, w_ref), (x_hbm, x_ref), (c_hbm, c_ref)))]
    for copy in fetch:
        copy.start()

    barrier = pltpu.get_barrier_semaphore()
    for k in range(1, ns):
        pl.semaphore_signal(barrier, inc=1, device_id={"space": lax.rem(s + k, ns)}, device_id_type=MESH)
    for k in range(1, nz):
        pl.semaphore_signal(barrier, inc=1, device_id={"tm": lax.rem(j + k, nz)}, device_id_type=MESH)
    slab = 16

    def turned(ref, at):
        return jnp.transpose(ref[pl.ds(pl.multiple_of(at, slab), slab)], (1, 0, 2))

    def turn_g(i, carry):
        gp[OWN, 1:rows + 1, pl.ds(pl.multiple_of(i * slab, slab), slab), :] = turned(g_ref, i * slab)
        return carry

    fetch[0].wait()
    lax.fori_loop(0, channels // slab, turn_g, 0)
    pl.semaphore_wait(barrier, ns - 1 + nz - 1)

    def row_copy(stream, slot_from, slot_to, r, target):
        src = gp.at[slot_from, r + 1]
        return pltpu.make_async_remote_copy(
            src_ref=src, dst_ref=gp.at[slot_to, r + 1],
            send_sem=z_send.at[stream, r], recv_sem=z_recv.at[slot_to, r],
            device_id={"tm": target}, device_id_type=MESH)

    prev = lax.rem(j + nz - 1, nz)
    nxt = lax.rem(j + 1, nz)

    def to_prev(r):
        return row_copy(TO_PREV, OWN, N1, r, prev)

    def fwd_prev(r):
        return row_copy(FWD_PREV, N1, N2, r, prev)

    def own_c0(r):
        return row_copy(TO_NEXT, OWN, C0, r, nxt)

    def own_c1(r):
        return row_copy(TO_NEXT, OWN, C1, r, nxt)

    def fwd_c1(r):
        return row_copy(FWD_C1, C1, C1, r, nxt)

    def fwd_c0(r):
        return row_copy(FWD_C0, C0, C0, r, nxt)

    for r in order:
        pl.when(j >= 1)(lambda: to_prev(r).start())
        pl.when(j == 0)(lambda: own_c0(r).start())
    pl.when(j == 1)(lambda: own_c1(order[0]).start())

    def halo_up(slot):
        src = gp.at[slot, 1]
        return pltpu.make_async_remote_copy(
            src_ref=src, dst_ref=gp.at[slot, rows + 1],
            send_sem=h_send.at[slot, 0], recv_sem=h_recv.at[slot, 0],
            device_id={"space": lax.rem(s + ns - 1, ns)}, device_id_type=MESH)

    def halo_down(slot):
        src = gp.at[slot, rows]
        return pltpu.make_async_remote_copy(
            src_ref=src, dst_ref=gp.at[slot, 0],
            send_sem=h_send.at[slot, 1], recv_sem=h_recv.at[slot, 1],
            device_id={"space": lax.rem(s + 1, ns)}, device_id_type=MESH)

    def halo_start_up(slot):
        pl.when(s >= 1)(lambda: halo_up(slot).start())

    def halo_start_down(slot):
        pl.when(s < ns - 1)(lambda: halo_down(slot).start())

    def halo_wait(slot):
        @pl.when(s >= 1)
        def _():
            halo_up(slot).wait_send()
            halo_down(slot).wait_recv()

        @pl.when(s < ns - 1)
        def _():
            halo_down(slot).wait_send()
            halo_up(slot).wait_recv()

    halo_start_up(OWN)
    halo_start_down(OWN)

    @pl.when(s == 0)
    def _():
        for slot in range(5):
            gp[slot, 0] = jnp.zeros(gp.shape[2:], gp.dtype)

    @pl.when(s == ns - 1)
    def _():
        for slot in range(5):
            gp[slot, rows + 1] = jnp.zeros(gp.shape[2:], gp.dtype)

    wtmp[...] = jnp.zeros_like(wtmp)
    acc[...] = jnp.zeros_like(acc)
    stack = xs_ref.shape[1]
    xs_ref[:, channels:, :] = jnp.zeros((rows, stack - channels, cols), xs_ref.dtype)
    wl_ref[:, channels:, :] = jnp.zeros((5, stack - channels, taps), wl_ref.dtype)
    fetch[1].wait()
    for slot, tap in ((OWN, 2), (N1, 1), (N2, 0)):
        flipped = jnp.concatenate(
            [w_ref[tap, (2 - b) * k_row:(3 - b) * k_row, :].astype(jnp.float32) for b in range(3)], axis=0)
        across_taps = flipped.T
        if tap < 2:
            wf[tap] = across_taps
        wl_ref[slot, :channels, :] = across_taps.astype(jnp.bfloat16)

    def share_of(tap):
        return wf[tap, pl.ds(pl.multiple_of(j * share, 8), share), :].astype(jnp.bfloat16)

    def turn_x(i, carry):
        xs_ref[:, pl.ds(pl.multiple_of(i * slab, slab), slab), :] = turned(x_ref, i * slab)
        return carry

    fetch[2].wait()
    lax.fori_loop(0, channels // slab, turn_x, 0)
    fetch[3].wait()
    xs_ref[:, channels:channels + share, :] = jnp.transpose(c_ref[0], (1, 0, 2))
    xs_ref[:, high:high + share, :] = jnp.transpose(c_ref[1], (1, 0, 2))
    for slot in (C1, C0):
        wl_ref[slot, :channels, :] = jnp.zeros((channels, taps), wl_ref.dtype)

    def weights_g0(slot):
        wl_ref[slot, channels:channels + share, :] = share_of(0)
        wl_ref[slot, high:high + share, :] = share_of(1)

    def weights_g1(slot):
        wl_ref[slot, high:high + share, :] = share_of(0)

    @pl.when(j == 0)
    def _():
        weights_g0(OWN)
        weights_g1(N1)

    pl.when(j == 1)(lambda: weights_g1(OWN))
    weights_g1(C1)
    weights_g0(C0)

    lane = lax.broadcasted_iota(jnp.int32, (channels, cols), 1)
    wide = 128
    wlane = lax.broadcasted_iota(jnp.int32, (taps, wide), 1)

    def shift_row(slot, p):
        value = gp[slot, p]
        full = value.astype(jnp.float32)
        ahead = jnp.where(lane == cols - 1, 0.0, pltpu.roll(full, cols - 1, 1))
        behind = jnp.where(lane == 0, 0.0, pltpu.roll(full, 1, 1))
        base = pl.multiple_of(p * k_row, 16)
        sc[pl.ds(base, channels), :] = ahead.astype(jnp.bfloat16)
        sc[pl.ds(pl.multiple_of(base + channels, 16), channels), :] = value
        sc[pl.ds(pl.multiple_of(base + 2 * channels, 16), channels), :] = behind.astype(jnp.bfloat16)

    def compute_row(slot, h):
        block = sc[pl.ds(pl.multiple_of(h * k_row, 16), taps), :]
        term = jnp.dot(wl_ref[slot], block, preferred_element_type=jnp.float32)
        if slot is OWN:
            dacc[h] = term
        else:
            dacc[h] += term
        wtmp[:, :stack] += lax.dot_general(
            block, xs_ref[h], (((1,), (1,)), ((), ())), preferred_element_type=jnp.float32)

    def placed_cache(block, shift_from):
        turned = pltpu.roll(block, lax.rem(j * share + 2 * wide - shift_from, wide), 1)
        inside = jnp.logical_and(wlane >= j * share, wlane < (j + 1) * share)
        return jnp.where(inside, turned, 0.0)

    def run(step, start, stop):
        def body(i, carry):
            step(i)
            return carry

        lax.fori_loop(start, stop, body, 0)

    def process(slot):
        run(functools.partial(shift_row, slot), 0, rows + 2)
        run(functools.partial(compute_row, slot), 0, rows)

    def add_x(tap):
        acc[tap, :taps, :] += jnp.where(wlane < channels, wtmp[:, :wide], 0.0)

    def add_g0():
        acc[0, :taps, :] += placed_cache(wtmp[:, :wide], channels)
        acc[1, :taps, :] += placed_cache(wtmp[:, wide:], 0)

    def add_g1():
        acc[0, :taps, :] += placed_cache(wtmp[:, wide:], 0)

    def clear():
        wtmp[...] = jnp.zeros_like(wtmp)

    def reduction(index):
        def rs_copy(k):
            to = lax.rem(s + k, ns)
            return pltpu.make_async_remote_copy(
                src_ref=sb.at[index, to], dst_ref=rb.at[index, s],
                send_sem=rs_send.at[index, k], recv_sem=rs_recv.at[index, s],
                device_id={"space": to}, device_id_type=MESH)

        def rs_landed(k):
            source = lax.rem(s + ns - k, ns)
            return pltpu.make_async_remote_copy(
                src_ref=sb.at[index, source], dst_ref=rb.at[index, source],
                send_sem=rs_send.at[index, k], recv_sem=rs_recv.at[index, source],
                device_id={"space": source}, device_id_type=MESH)

        def z_copy(k):
            return pltpu.make_async_remote_copy(
                src_ref=zs.at[index], dst_ref=zb.at[index, j],
                send_sem=zz_send.at[index, k], recv_sem=zz_recv.at[index, j],
                device_id={"tm": lax.rem(j + k, nz)}, device_id_type=MESH)

        def z_landed(k):
            source = lax.rem(j + nz - k, nz)
            return pltpu.make_async_remote_copy(
                src_ref=zs.at[index], dst_ref=zb.at[index, source],
                send_sem=zz_send.at[index, k], recv_sem=zz_recv.at[index, source],
                device_id={"tm": source}, device_id_type=MESH)

        def ag_copy(k):
            return pltpu.make_async_remote_copy(
                src_ref=gb.at[index, s], dst_ref=gb.at[index, s],
                send_sem=ag_send.at[index, k], recv_sem=ag_recv.at[index, s],
                device_id={"space": lax.rem(s + k, ns)}, device_id_type=MESH)

        def ag_landed(k):
            source = lax.rem(s + ns - k, ns)
            return pltpu.make_async_remote_copy(
                src_ref=gb.at[index, source], dst_ref=gb.at[index, source],
                send_sem=ag_send.at[index, k], recv_sem=ag_recv.at[index, source],
                device_id={"space": source}, device_id_type=MESH)

        def scatter():
            for q in range(ns):
                sb[index, q] = acc[index, q * ck:(q + 1) * ck, :].astype(jnp.bfloat16)
            for k in range(1, ns):
                rs_copy(k).start()

        def across():
            total = acc[index, pl.ds(pl.multiple_of(s * ck, 16), ck), :]
            for k in range(1, ns):
                rs_landed(k).wait_recv()
                total = total + rb[index, lax.rem(s + ns - k, ns)].astype(jnp.float32)
            zs[index] = total.astype(jnp.bfloat16)
            for k in range(1, nz):
                z_copy(k).start()

        def gather():
            zb[index, j] = zs[index]
            for k in range(1, nz):
                z_landed(k).wait_recv()
            total = zb[index, 0].astype(jnp.float32)
            for q in range(1, nz):
                total = total + zb[index, q].astype(jnp.float32)
            gb[index, s] = total.astype(jnp.bfloat16)
            for k in range(1, ns):
                ag_copy(k).start()

        def finish():
            for k in range(1, ns):
                ag_landed(k).wait_recv()
            for q in range(ns):
                acc[index, q * ck:(q + 1) * ck, :] = gb[index, q].astype(jnp.float32)
            for b in range(3):
                for d in range(3):
                    at = (b * 3 + d) * channels
                    wg_ref[index, 2 - b, d] = acc[index, at:at + channels, :channels] * scale
            for k in range(1, ns):
                rs_copy(k).wait_send()
                ag_copy(k).wait_send()
            for k in range(1, nz):
                z_copy(k).wait_send()

        return scatter, across, gather, finish

    steps = [reduction(tap) for tap in range(3)]
    scatter, across, gather, finish = range(4)

    has_n1 = j < last
    passes_on = j < last

    def c1_row(r):
        @pl.when(j >= 2)
        def _():
            own_c1(r).wait_recv()
            pl.when(passes_on)(lambda: fwd_c1(r).start())

    def halo_after(slot, r):
        if r == 0:
            halo_start_up(slot)
        if r == rows - 1:
            halo_start_down(slot)

    def c0_row(r):
        own_c0(r).wait_recv()
        pl.when(passes_on)(lambda: fwd_c0(r).start())
        halo_after(C0, r)

    c1_row(order[0])
    pl.when(j == 1)(lambda: c0_row(order[0]))
    halo_wait(OWN)
    process(OWN)
    add_x(2)
    steps[2][scatter]()
    pl.when(j == 0)(add_g0)
    pl.when(j == 1)(add_g1)
    clear()

    for count, r in enumerate(order):
        pl.when(j >= (2 if count == 0 else 1))(lambda: c0_row(r))

        @pl.when(has_n1)
        def _():
            to_prev(r).wait_recv()
            pl.when(j >= 1)(lambda: fwd_prev(r).start())
            halo_after(N1, r)


    @pl.when(j == 1)
    def _():
        for r in order[1:]:
            own_c1(r).start()

    @pl.when(has_n1)
    def _():
        halo_wait(N1)
        process(N1)
        add_x(1)
        pl.when(j == 0)(add_g1)
        clear()

    c1_row(order[1])

    @pl.when(j >= 1)
    def _():
        halo_wait(C0)
        process(C0)
        add_g0()
        clear()

    steps[1][scatter]()
    for r in order[2:-1]:
        c1_row(r)

    def late_row(r):
        row_copy(FWD_PREV, N1, late, r, prev).wait_recv()

    for r in order[:-1]:
        @pl.when(j < last - 1)
        def _():
            late_row(r)

        halo_after(late, r)
    missing = order[-1] + 1
    halo_wait(late)
    run(functools.partial(shift_row, late), 0, missing)
    run(functools.partial(shift_row, late), missing + 1, rows + 2)
    run(functools.partial(compute_row, late), 0, missing - 2)
    c1_row(order[-1])
    steps[2][across]()
    steps[1][across]()

    @pl.when(j < last - 1)
    def _():
        late_row(order[-1])

    shift_row(late, missing)
    run(functools.partial(compute_row, late), missing - 2, rows)
    pl.when(j < last - 1)(lambda: add_x(0))
    pl.when(j >= last - 1)(add_g1)
    steps[0][scatter]()
    steps[2][gather]()
    steps[1][gather]()

    def turn_out(i, carry):
        at = pl.ds(pl.multiple_of(i * slab, slab), slab)
        ig_ref[at] = jnp.transpose(dacc[:, at, :].astype(jnp.bfloat16), (1, 0, 2))
        return carry

    lax.fori_loop(0, channels // slab, turn_out, 0)
    cg_ref[0] = jnp.transpose(dacc[:, channels:channels + share, :].astype(jnp.bfloat16), (1, 0, 2))
    cg_ref[1] = jnp.transpose(dacc[:, high:high + share, :].astype(jnp.bfloat16), (1, 0, 2))
    steps[0][across]()
    steps[2][finish]()
    steps[1][finish]()
    steps[0][gather]()

    for r in range(rows):
        @pl.when(j >= 1)
        def _():
            to_prev(r).wait_send()

        @pl.when(jnp.logical_and(j >= 1, has_n1))
        def _():
            fwd_prev(r).wait_send()

        @pl.when(j == 0)
        def _():
            own_c0(r).wait_send()

        @pl.when(j == 1)
        def _():
            own_c1(r).wait_send()

        @pl.when(jnp.logical_and(j >= 1, passes_on))
        def _():
            fwd_c0(r).wait_send()

        @pl.when(jnp.logical_and(j >= 2, passes_on))
        def _():
            fwd_c1(r).wait_send()
    steps[0][finish]()


def up_to(value, step):
    return -(-value // step) * step


def per_device(nz, ns, frames, cache, grad_out, weight):
    _, channels, rows, cols = frames.shape
    share = cache.shape[1]
    taps = 9 * channels
    stack = 128 + up_to(share, 32)
    ck = up_to(-(-taps // ns), 16)
    scale = 1.0 / math.sqrt(nz * ns * rows * cols)
    f32, bf16 = jnp.float32, jnp.bfloat16
    vmem = pl.BlockSpec(memory_space=pltpu.VMEM)
    hbm = pl.BlockSpec(memory_space=pl.ANY)
    dma = pltpu.SemaphoreType.DMA
    ig, cg, weight_grad = pl.pallas_call(
        functools.partial(kernel, nz, ns, ck, channels, share, scale),
        out_shape=(
            jax.ShapeDtypeStruct(frames.shape[1:], bf16),
            jax.ShapeDtypeStruct(cache.shape, bf16),
            jax.ShapeDtypeStruct(weight.shape, f32),
        ),
        in_specs=[hbm] * 4,
        out_specs=(vmem,) * 3,
        scratch_shapes=[
            pltpu.VMEM(frames.shape[1:], bf16),
            pltpu.VMEM(frames.shape[1:], bf16),
            pltpu.VMEM(cache.shape, bf16),
            pltpu.VMEM((3, taps, channels), bf16),
            pltpu.VMEM((2, channels, taps), f32),
            pltpu.VMEM((5, rows + 2, channels, cols), bf16),
            pltpu.VMEM(((rows + 2) * 3 * channels, cols), bf16),
            pltpu.VMEM((rows, stack, cols), f32),
            pltpu.VMEM((taps, 256), f32),
            pltpu.VMEM((3, ns * ck, 128), f32),
            pltpu.VMEM((rows, stack, cols), bf16),
            pltpu.VMEM((5, stack, taps), bf16),
            pltpu.VMEM((3, ns, ck, 128), bf16), pltpu.VMEM((3, ns, ck, 128), bf16),
            pltpu.VMEM((3, ck, 128), bf16), pltpu.VMEM((3, nz, ck, 128), bf16),
            pltpu.VMEM((3, ns, ck, 128), bf16),
            dma((4,)),
            dma((5, rows)), dma((5, rows)), dma((5, 2)), dma((5, 2)),
            dma((3, ns)), dma((3, ns)), dma((3, nz)), dma((3, nz)), dma((3, ns)), dma((3, ns)),
        ],
        compiler_params=pltpu.CompilerParams(
            collective_id=0, has_side_effects=True, vmem_limit_bytes=60 * 1024 * 1024),
    )(grad_out[0], frames[0], cache, weight.reshape(3, taps, channels))
    return ig[None], cg, weight_grad


def solution(mesh):
    placed = (
        P("tm", None, "space", None),
        P(None, "tm", "space", None),
        P("tm", None, "space", None),
        P(),
    )
    return jax.shard_map(
        functools.partial(per_device, mesh.shape["tm"], mesh.shape["space"]),
        mesh=mesh,
        in_specs=placed,
        out_specs=(P("tm", None, "space", None), P(None, "tm", "space", None), P()),
        check_vma=False,
    )
```

```python
import functools
import math

import jax
import jax.numpy as jnp
from jax import lax
from jax.experimental import pallas as pl
from jax.experimental.pallas import tpu as pltpu
from jax.sharding import PartitionSpec as P

MESH = pl.DeviceIdType.MESH
OWN, N1, LATE, C0 = range(4)
TO_PREV, FWD_PREV, TO_NEXT, FWD_C0 = range(4)
NT = (((1,), (1,)), ((), ()))
LANES = 128
F32, BF16 = jnp.float32, jnp.bfloat16


def kernel(
    nz, ns, ck, scale,
    g_hbm, x_hbm, c_hbm, w_hbm, ig_ref, cg_ref, wg_ref,
    g_ref, x_ref, c_ref, w_ref,
    gp, sc, xpad, cpad, dx, dc, wlx, wlc, wtx, wtc, flat,
    sb, rb, zs, zb, gb, cb, res_out, res_in,
    loads, z_send, z_recv, h_send, h_recv,
    rs_send, rs_recv, zz_send, zz_recv, ag_send, ag_recv, c_sem, res_sem,
):
    assert nz == 4
    j = lax.axis_index("tm")
    s = lax.axis_index("space")
    channels, rows, cols = g_ref.shape
    share = c_ref.shape[1]
    half = 2 * share
    assert channels == 2 * half and rows >= 4
    width = 3 * channels
    full, rem = width // LANES, width % LANES
    groups = LANES // rem
    part = width // groups
    assert full == 2 and LANES % rem == 0 and part % 8 == 0
    last = nz - 1
    order = [0, rows - 1, *range(1, rows - 1)]
    slab = 16
    prev = lax.rem(j + nz - 1, nz)
    nxt = lax.rem(j + 1, nz)

    def both(*terms):
        return functools.reduce(jnp.logical_and, terms)

    def ordered(i):
        return jnp.where(i == 0, 0, jnp.where(i == 1, rows - 1, i - 1))

    fetch_g, fetch_c, fetch_x, fetch_w = [
        pltpu.make_async_copy(src, dst, loads.at[n])
        for n, (src, dst) in enumerate(((g_hbm, g_ref), (c_hbm, c_ref), (x_hbm, x_ref), (w_hbm, w_ref)))]
    for copy in (fetch_g, fetch_c, fetch_x, fetch_w):
        copy.start()
    barrier = pltpu.get_barrier_semaphore()
    for k in range(1, ns):
        pl.semaphore_signal(barrier, inc=1, device_id={"space": lax.rem(s + k, ns)}, device_id_type=MESH)
    for k in range(1, nz):
        pl.semaphore_signal(barrier, inc=1, device_id={"tm": lax.rem(j + k, nz)}, device_id_type=MESH)

    def turned(ref, at):
        return jnp.transpose(ref[pl.ds(pl.multiple_of(at, slab), slab)], (1, 0, 2))

    def turn_g(i, carry):
        gp[OWN, 1:rows + 1, pl.ds(pl.multiple_of(i * slab, slab), slab), :] = turned(g_ref, i * slab)
        return carry

    fetch_g.wait()
    lax.fori_loop(0, channels // slab, turn_g, 0)
    fetch_c.wait()
    pl.semaphore_wait(barrier, ns - 1 + nz - 1)

    def row_copy(stream, slot_from, slot_to, r, target):
        return pltpu.make_async_remote_copy(
            src_ref=gp.at[slot_from, r + 1], dst_ref=gp.at[slot_to, r + 1],
            send_sem=z_send.at[stream, r], recv_sem=z_recv.at[slot_to, r],
            device_id={"tm": target}, device_id_type=MESH)

    def to_prev(r):
        return row_copy(TO_PREV, OWN, N1, r, prev)

    def fwd_prev(r):
        return row_copy(FWD_PREV, N1, LATE, r, prev)

    def own_c0(r):
        return row_copy(TO_NEXT, OWN, C0, r, nxt)

    def own_c1(r):
        return row_copy(TO_NEXT, OWN, LATE, r, nxt)

    def fwd_c0(r):
        return row_copy(FWD_C0, C0, C0, r, nxt)

    def cache_copy():
        return pltpu.make_async_remote_copy(
            src_ref=c_ref, dst_ref=cb, send_sem=c_sem.at[0], recv_sem=c_sem.at[1],
            device_id={"tm": prev}, device_id_type=MESH)

    def result_copy(f):
        return pltpu.make_async_remote_copy(
            src_ref=res_out.at[f], dst_ref=res_in.at[f], send_sem=res_sem.at[0, f], recv_sem=res_sem.at[1, f],
            device_id={"tm": nxt}, device_id_type=MESH)

    pl.when(j == last)(lambda: cache_copy().start())
    for i, r in enumerate(order):
        pl.when(j >= 1)(lambda: to_prev(r).start())
        pl.when(j == 0)(lambda: own_c0(r).start())
        if i < 2:
            pl.when(j == 1)(lambda: own_c1(r).start())

    def halo_up(slot):
        return pltpu.make_async_remote_copy(
            src_ref=gp.at[slot, 1], dst_ref=gp.at[slot, rows + 1],
            send_sem=h_send.at[slot, 0], recv_sem=h_recv.at[slot, 0],
            device_id={"space": lax.rem(s + ns - 1, ns)}, device_id_type=MESH)

    def halo_down(slot):
        return pltpu.make_async_remote_copy(
            src_ref=gp.at[slot, rows], dst_ref=gp.at[slot, 0],
            send_sem=h_send.at[slot, 1], recv_sem=h_recv.at[slot, 1],
            device_id={"space": lax.rem(s + 1, ns)}, device_id_type=MESH)

    def halo_start(slot, i):
        pl.when(both(i == 0, s >= 1))(lambda: halo_up(slot).start())
        pl.when(both(i == 1, s < ns - 1))(lambda: halo_down(slot).start())

    for i in range(2):
        halo_start(OWN, jnp.int32(i))

    edge = 2 * channels
    for ref in (xpad, cpad):
        ref[:edge, :] = jnp.zeros((edge, cols), BF16)
        ref[edge + rows * channels:, :] = jnp.zeros((edge, cols), BF16)
    dx[...] = jnp.zeros_like(dx)
    dc[...] = jnp.zeros_like(dc)
    wtx[...] = jnp.zeros_like(wtx)
    wtc[...] = jnp.zeros_like(wtc)
    used = full * width + part
    for tap in range(3):
        flat[tap, used:, :] = jnp.zeros((ns * ck - used, LANES), F32)

    def turn_x(i, carry):
        block = turned(x_ref, i * slab)
        for h in range(rows):
            xpad[pl.ds(pl.multiple_of((h + 2) * channels + i * slab, slab), slab), :] = block[h]
        return carry

    fetch_x.wait()
    lax.fori_loop(0, channels // slab, turn_x, 0)

    def turn_w(i, carry):
        at = pl.multiple_of(lax.rem(i, 3) * channels, slab)
        wlx[lax.div(i, 3), pl.ds(at, channels), :] = w_ref[i].astype(F32).T.astype(BF16)
        return carry

    fetch_w.wait()
    lax.fori_loop(0, 9, turn_w, 0)
    base = jnp.where(j < 2, 0, half)
    for b in range(3):
        at = b * channels
        near = pl.ds(pl.multiple_of(at + base, slab), half)
        wlc[0, at:at + half, :] = wlx[0, near, :]
        wlc[0, at + half:at + channels, :] = wlx[1, near, :]
        wlc[1, at:at + half, :] = jnp.zeros((half, width), BF16)
        wlc[1, at + half:at + channels, :] = wlx[0, near, :]

    def place_cache(lower, upper):
        nothing = jnp.zeros((rows, share, cols), F32)
        for f in range(2):
            low, high = [
                nothing if ref is None else jnp.transpose(ref[f].astype(F32), (1, 0, 2)) for ref in (lower, upper)]
            for h in range(rows):
                at = (h + 2) * channels + f * half
                cpad[at:at + half, :] = jnp.concatenate([low[h], high[h]], axis=0).astype(BF16)

    pl.when(j == 0)(lambda: place_cache(c_ref, None))
    pl.when(j == 1)(lambda: place_cache(None, c_ref))

    lane = lax.broadcasted_iota(jnp.int32, (channels, cols), 1)

    def shift(slot, p, to):
        value = gp[slot, p]
        wide = value.astype(F32)
        sc[to, :channels, :] = jnp.where(lane == cols - 1, 0.0, pltpu.roll(wide, cols - 1, 1)).astype(BF16)
        sc[to, channels:2 * channels, :] = value
        sc[to, 2 * channels:, :] = jnp.where(lane == 0, 0.0, pltpu.roll(wide, 1, 1)).astype(BF16)

    def kernel_sum(wt, pad, index, at, p):
        span = pl.ds(pl.multiple_of(p * channels, slab), width)
        wt[index, :, :width] += lax.dot_general(sc[at], pad[span, :], NT, preferred_element_type=F32)

    def data_sum(wl, out, index, at, p):
        span = pl.ds(pl.multiple_of(p * channels, slab), width)
        out[span, :] += jnp.dot(wl[index], sc[at], preferred_element_type=F32)

    def halo_sums(wt, pad, wl, out, index, at, side):
        h, b = (0, 2) if side == 0 else (rows - 1, 0)
        span = slice((h + 2) * channels, (h + 3) * channels)
        tap = slice(b * channels, (b + 1) * channels)
        wt[index, :, tap] += lax.dot_general(sc[at], pad[span, :], NT, preferred_element_type=F32)
        out[span, :] += jnp.dot(wl[index, tap, :], sc[at], preferred_element_type=F32)

    wide_lane = lax.broadcasted_iota(jnp.int32, (width, wtx.shape[2]), 1)
    in_lower = both(lax.rem(wide_lane, channels) < half, wide_lane < width)
    in_upper = both(lax.rem(wide_lane, channels) >= half, wide_lane < width)
    back = wtx.shape[2] - half

    def pack(tap):
        def put(total):
            for q in range(full):
                flat[tap, q * width:(q + 1) * width, :] = total[:, q * LANES:(q + 1) * LANES]
            tail = total[:, full * LANES:]
            packed = tail[:part]
            for k in range(1, groups):
                packed = packed + pltpu.roll(tail[k * part:(k + 1) * part], k * rem, 1)
            flat[tap, full * width:used, :] = packed

        own = wtx[tap]
        if tap == 2:
            put(own)
            return

        @pl.when(j < 2)
        def _():
            turned_c0 = pltpu.roll(wtc[0], back, 1)
            put(own + jnp.where(
                in_lower, turned_c0 if tap == 1 else wtc[0] + pltpu.roll(wtc[1], back, 1), 0.0))

        @pl.when(j >= 2)
        def _():
            put(own + jnp.where(in_upper, wtc[0] if tap == 1 else pltpu.roll(wtc[0], half, 1) + wtc[1], 0.0))

    def reduction(index):
        def rs_copy(k):
            to = lax.rem(s + k, ns)
            return pltpu.make_async_remote_copy(
                src_ref=sb.at[index, to], dst_ref=rb.at[index, s],
                send_sem=rs_send.at[index, k], recv_sem=rs_recv.at[index, s],
                device_id={"space": to}, device_id_type=MESH)

        def rs_landed(k):
            source = lax.rem(s + ns - k, ns)
            return pltpu.make_async_remote_copy(
                src_ref=sb.at[index, source], dst_ref=rb.at[index, source],
                send_sem=rs_send.at[index, k], recv_sem=rs_recv.at[index, source],
                device_id={"space": source}, device_id_type=MESH)

        def z_copy(k):
            return pltpu.make_async_remote_copy(
                src_ref=zs.at[index], dst_ref=zb.at[index, j],
                send_sem=zz_send.at[index, k], recv_sem=zz_recv.at[index, j],
                device_id={"tm": lax.rem(j + k, nz)}, device_id_type=MESH)

        def z_landed(k):
            source = lax.rem(j + nz - k, nz)
            return pltpu.make_async_remote_copy(
                src_ref=zs.at[index], dst_ref=zb.at[index, source],
                send_sem=zz_send.at[index, k], recv_sem=zz_recv.at[index, source],
                device_id={"tm": source}, device_id_type=MESH)

        def ag_copy(k):
            return pltpu.make_async_remote_copy(
                src_ref=gb.at[index, s], dst_ref=gb.at[index, s],
                send_sem=ag_send.at[index, k], recv_sem=ag_recv.at[index, s],
                device_id={"space": lax.rem(s + k, ns)}, device_id_type=MESH)

        def ag_landed(k):
            source = lax.rem(s + ns - k, ns)
            return pltpu.make_async_remote_copy(
                src_ref=gb.at[index, source], dst_ref=gb.at[index, source],
                send_sem=ag_send.at[index, k], recv_sem=ag_recv.at[index, source],
                device_id={"space": source}, device_id_type=MESH)

        def scatter():
            pack(index)
            for q in range(ns):
                sb[index, q] = flat[index, q * ck:(q + 1) * ck, :].astype(BF16)
            for k in range(1, ns):
                rs_copy(k).start()

        def across():
            total = flat[index, pl.ds(pl.multiple_of(s * ck, slab), ck), :]
            for k in range(1, ns):
                rs_landed(k).wait_recv()
                total = total + rb[index, lax.rem(s + ns - k, ns)].astype(F32)
            zs[index] = total.astype(BF16)

        def exchange():
            for k in range(1, nz):
                z_copy(k).start()

        def gather():
            zb[index, j] = zs[index]
            for k in range(1, nz):
                z_landed(k).wait_recv()
            total = zb[index, 0].astype(F32)
            for q in range(1, nz):
                total = total + zb[index, q].astype(F32)
            gb[index, s] = total.astype(BF16)
            for k in range(1, ns):
                ag_copy(k).start()

        def finish():
            for k in range(1, ns):
                ag_landed(k).wait_recv()
            for q in range(ns):
                flat[index, q * ck:(q + 1) * ck, :] = gb[index, q].astype(F32) * scale
            first = flat[index, :width, :]
            second = flat[index, width:2 * width, :]
            packed = flat[index, 2 * width:used, :]
            at = lax.broadcasted_iota(jnp.int32, (width, LANES), 1)
            step = LANES - channels
            middle = jnp.where(at < step, pltpu.roll(first, step, 1), pltpu.roll(second, step, 1))
            third = jnp.concatenate(
                [pltpu.roll(packed, (2 * step - k * rem) % LANES, 1) if (2 * step - k * rem) % LANES else packed
                 for k in range(groups)], axis=0)
            final = jnp.where(at < 2 * step, pltpu.roll(second, 2 * step, 1), third)
            for b, value in enumerate((first, middle, final)):
                wg_ref[index, b] = value[:, :channels]

        def sent():
            for k in range(1, ns):
                rs_copy(k).wait_send()
                ag_copy(k).wait_send()
            for k in range(1, nz):
                z_copy(k).wait_send()

        return scatter, across, exchange, gather, finish, sent

    steps = [reduction(tap) for tap in range(3)]
    scatter, across, exchange, gather, finish, sent = range(6)

    def middle_row(e):
        r = ordered(e)

        @pl.when(j < last)
        def _():
            row_copy(TO_PREV, OWN, N1, r, prev).wait_recv()
            pl.when(j >= 1)(lambda: fwd_prev(r).start())
            halo_start(N1, e)

        @pl.when(both(j >= 1, j < last))
        def _():
            row_copy(TO_NEXT, OWN, C0, r, nxt).wait_recv()
            pl.when(j == 1)(lambda: fwd_c0(r).start())
            halo_start(C0, e)

        @pl.when(both(j == 1, e == rows - 1))
        def _():
            for q in order[2:]:
                own_c1(q).start()

    def late_row(e):
        @pl.when(j < last)
        def _():
            row_copy(FWD_PREV, N1, LATE, ordered(e), prev).wait_recv()
            halo_start(LATE, e)

    def halo_wait(slot, side):
        if side == 0:
            halo_up(slot).wait_send()
            halo_down(slot).wait_recv()
        else:
            halo_down(slot).wait_send()
            halo_up(slot).wait_recv()

    ahead = jnp.where(j < 2, 1, 0)

    def results(f, offset):
        rows_of = [
            dc[pl.ds(pl.multiple_of((h + 2) * channels + f * half + offset, 8), share), :] for h in range(rows)]
        return jnp.transpose(jnp.stack(rows_of, axis=0).astype(BF16), (1, 0, 2))

    def step(n, carry):
        phase = lax.div(n, rows)
        i = lax.rem(n, rows)
        r = ordered(i)

        @pl.when(both(n >= rows, n + ahead < 2 * rows))
        def _():
            middle_row(n + ahead - rows)

        pl.when(phase == 2)(lambda: late_row(i))

        @pl.when(both(n == rows, j == 2))
        def _():
            cache_copy().wait_recv()
            place_cache(c_ref, cb)

        with_x = jnp.logical_or(phase == 0, jnp.logical_or(both(phase == 1, j < last), j < 2))
        x_slot = phase
        tap = 2 - phase
        with_c = jnp.logical_or(
            both(phase == 0, j < 2), jnp.logical_or(both(phase == 1, j < last), both(phase == 2, j == 2)))
        apart = both(phase >= 1, j >= 1)
        c_slot = jnp.where(apart, jnp.where(phase == 1, C0, LATE), phase)
        c_kind = jnp.where(phase == 0, j, jnp.where(both(phase == 1, j >= 1), 0, 1))
        c_at = jnp.where(apart, 1, 0)

        @pl.when(with_x)
        def _():
            shift(x_slot, r + 1, 0)
            kernel_sum(wtx, xpad, tap, 0, r + 1)
            data_sum(wlx, dx, tap, 0, r + 1)

        @pl.when(with_c)
        def _():
            pl.when(apart)(lambda: shift(c_slot, r + 1, 1))
            kernel_sum(wtc, cpad, c_kind, c_at, r + 1)
            data_sum(wlc, dc, c_kind, c_at, r + 1)

        pl.when(both(n == 2, j < 2))(lambda: middle_row(jnp.int32(0)))

        @pl.when(i == 2)
        def _():
            for side in range(2):
                p = 0 if side == 0 else rows + 1

                @pl.when(s >= 1 if side == 0 else s < ns - 1)
                def _():
                    @pl.when(with_x)
                    def _():
                        halo_wait(x_slot, side)
                        shift(x_slot, p, 0)
                        halo_sums(wtx, xpad, wlx, dx, tap, 0, side)

                    @pl.when(with_c)
                    def _():
                        @pl.when(apart)
                        def _():
                            halo_wait(c_slot, side)
                            shift(c_slot, p, 1)

                        halo_sums(wtc, cpad, wlc, dc, c_kind, c_at, side)

        pl.when(n == rows - 1)(steps[2][scatter])

        @pl.when(n == 2 * rows - 1)
        def _():
            steps[1][scatter]()

            @pl.when(j == 2)
            def _():
                res_out[0] = results(0, share)
                result_copy(0).start()

        return carry

    lax.fori_loop(0, 3 * rows - 1, step, 0)
    steps[2][across]()
    steps[1][across]()

    final = jnp.int32(rows - 1)
    p = order[-1] + 1
    late_row(final)

    @pl.when(j < 2)
    def _():
        shift(LATE, p, 0)
        kernel_sum(wtx, xpad, 0, 0, p)

    @pl.when(j == 2)
    def _():
        shift(LATE, p, 1)
        kernel_sum(wtc, cpad, 1, 1, p)

    steps[0][scatter]()
    steps[2][exchange]()
    steps[1][exchange]()

    @pl.when(j == 2)
    def _():
        data_sum(wlc, dc, 1, 1, p)
        res_out[1] = results(1, share)
        result_copy(1).start()

    pl.when(j < 2)(lambda: data_sum(wlx, dx, 0, 0, p))

    def turn_out(i, carry):
        block = [
            dx[pl.ds(pl.multiple_of((h + 2) * channels + i * slab, slab), slab), :] for h in range(rows)]
        ig_ref[pl.ds(pl.multiple_of(i * slab, slab), slab)] = jnp.transpose(
            jnp.stack(block, axis=0).astype(BF16), (1, 0, 2))
        return carry

    lax.fori_loop(0, channels // slab, turn_out, 0)

    @pl.when(j < last)
    def _():
        offset = jnp.where(j == 1, share, 0)
        for f in range(2):
            cg_ref[f] = results(f, offset)

    steps[0][across]()
    steps[0][exchange]()
    steps[2][gather]()
    steps[1][gather]()
    steps[0][gather]()
    steps[2][finish]()
    steps[1][finish]()

    @pl.when(j == last)
    def _():
        for f in range(2):
            result_copy(f).wait_recv()
            cg_ref[f] = res_in[f]
        cache_copy().wait_send()

    @pl.when(j == 2)
    def _():
        for f in range(2):
            result_copy(f).wait_send()

    for r in range(rows):
        pl.when(j >= 1)(lambda: to_prev(r).wait_send())
        pl.when(both(j >= 1, j < last))(lambda: fwd_prev(r).wait_send())
        pl.when(j == 0)(lambda: own_c0(r).wait_send())

        @pl.when(j == 1)
        def _():
            own_c1(r).wait_send()
            fwd_c0(r).wait_send()

    for tap in range(3):
        steps[tap][sent]()
    steps[0][finish]()


def up_to(value, step):
    return -(-value // step) * step


def per_device(nz, ns, frames, cache, grad_out, weight):
    _, channels, rows, cols = frames.shape
    width = 3 * channels
    wide = up_to(width, LANES)
    ck = up_to(-(-(width * channels * 3) // (ns * LANES)), 16)
    scale = 1.0 / math.sqrt(nz * ns * rows * cols)
    vmem = pl.BlockSpec(memory_space=pltpu.VMEM)
    hbm = pl.BlockSpec(memory_space=pl.ANY)
    dma = pltpu.SemaphoreType.DMA
    padded = (rows + 4) * channels
    ig, cg, weight_grad = pl.pallas_call(
        functools.partial(kernel, nz, ns, ck, scale),
        out_shape=(
            jax.ShapeDtypeStruct(frames.shape[1:], BF16),
            jax.ShapeDtypeStruct(cache.shape, BF16),
            jax.ShapeDtypeStruct((3, 3, width, channels), F32),
        ),
        in_specs=[hbm] * 4,
        out_specs=(vmem,) * 3,
        scratch_shapes=[
            pltpu.VMEM(frames.shape[1:], BF16),
            pltpu.VMEM(frames.shape[1:], BF16),
            pltpu.VMEM(cache.shape, BF16),
            pltpu.VMEM((9, width, channels), BF16),
            pltpu.VMEM((4, rows + 2, channels, cols), BF16),
            pltpu.VMEM((2, width, cols), BF16),
            pltpu.VMEM((padded, cols), BF16), pltpu.VMEM((padded, cols), BF16),
            pltpu.VMEM((padded, cols), F32), pltpu.VMEM((padded, cols), F32),
            pltpu.VMEM((3, width, width), BF16), pltpu.VMEM((2, width, width), BF16),
            pltpu.VMEM((3, width, wide), F32), pltpu.VMEM((2, width, wide), F32),
            pltpu.VMEM((3, ns * ck, LANES), F32),
            pltpu.VMEM((3, ns, ck, LANES), BF16), pltpu.VMEM((3, ns, ck, LANES), BF16),
            pltpu.VMEM((3, ck, LANES), BF16), pltpu.VMEM((3, nz, ck, LANES), BF16),
            pltpu.VMEM((3, ns, ck, LANES), BF16),
            pltpu.VMEM(cache.shape, BF16), pltpu.VMEM(cache.shape, BF16), pltpu.VMEM(cache.shape, BF16),
            dma((4,)),
            dma((4, rows)), dma((4, rows)), dma((4, 2)), dma((4, 2)),
            dma((3, ns)), dma((3, ns)), dma((3, nz)), dma((3, nz)), dma((3, ns)), dma((3, ns)),
            dma((2,)), dma((2, 2)),
        ],
        compiler_params=pltpu.CompilerParams(
            collective_id=0, has_side_effects=True, vmem_limit_bytes=60 * 1024 * 1024),
    )(grad_out[0], frames[0], cache, weight.reshape(9, width, channels))
    return ig[None], cg, weight_grad.reshape(weight.shape)


def solution(mesh):
    placed = (
        P("tm", None, "space", None),
        P(None, "tm", "space", None),
        P("tm", None, "space", None),
        P(),
    )
    return jax.shard_map(
        functools.partial(per_device, mesh.shape["tm"], mesh.shape["space"]),
        mesh=mesh,
        in_specs=placed,
        out_specs=(P("tm", None, "space", None), P(None, "tm", "space", None), P()),
        check_vma=False,
    )
```

```python
import functools
import math

import jax
import jax.numpy as jnp
from jax import lax
from jax.experimental import pallas as pl
from jax.experimental.pallas import tpu as pltpu
from jax.sharding import PartitionSpec as P

MESH = pl.DeviceIdType.MESH
OWN, N1, LATE, C0 = range(4)
TO_PREV, FWD_PREV, TO_NEXT, FWD_C0 = range(4)
NT = (((1,), (1,)), ((), ()))
LANES = 128
F32, BF16 = jnp.float32, jnp.bfloat16


def kernel(
    nz, ns, ck,
    g_hbm, x_hbm, c_hbm, w_hbm, ig_hbm, cg_hbm, gb,
    ig_ref, cg_ref, g_ref, x_ref, c_ref, w_ref,
    gp, sc, xpad, cpad, dx, dc, wlx, wlc, wtx, wtc, flat,
    sb, rb, zs, zb, mine, cb, res_out, res_in,
    loads, z_send, z_recv, h_send, h_recv,
    rs_send, rs_recv, zz_send, zz_recv, ag_send, ag_recv, c_sem, res_sem, stores,
):
    assert nz == 4
    j = lax.axis_index("tm")
    s = lax.axis_index("space")
    channels, rows, cols = g_ref.shape
    share = c_ref.shape[1]
    half = 2 * share
    assert channels == 2 * half and rows >= 4
    width = 3 * channels
    full, rem = width // LANES, width % LANES
    groups = LANES // rem
    part = width // groups
    assert full == 2 and LANES % rem == 0 and part % 8 == 0
    last = nz - 1
    order = [0, rows - 1, *range(1, rows - 1)]
    slab = 16
    prev = lax.rem(j + nz - 1, nz)
    nxt = lax.rem(j + 1, nz)

    def both(*terms):
        return functools.reduce(jnp.logical_and, terms)

    def ordered(i):
        return jnp.where(i == 0, 0, jnp.where(i == 1, rows - 1, i - 1))

    fetch_g, fetch_c, fetch_x, fetch_w = [
        pltpu.make_async_copy(src, dst, loads.at[n])
        for n, (src, dst) in enumerate(((g_hbm, g_ref), (c_hbm, c_ref), (x_hbm, x_ref), (w_hbm, w_ref)))]
    for copy in (fetch_g, fetch_c, fetch_x, fetch_w):
        copy.start()
    barrier = pltpu.get_barrier_semaphore()
    for k in range(1, ns):
        pl.semaphore_signal(barrier, inc=1, device_id={"space": lax.rem(s + k, ns)}, device_id_type=MESH)
    for k in range(1, nz):
        pl.semaphore_signal(barrier, inc=1, device_id={"tm": lax.rem(j + k, nz)}, device_id_type=MESH)

    def turned(ref, at):
        return jnp.transpose(ref[pl.ds(pl.multiple_of(at, slab), slab)], (1, 0, 2))

    def turn_g(i, carry):
        gp[OWN, 1:rows + 1, pl.ds(pl.multiple_of(i * slab, slab), slab), :] = turned(g_ref, i * slab)
        return carry

    fetch_g.wait()
    lax.fori_loop(0, channels // slab, turn_g, 0)
    fetch_c.wait()
    pl.semaphore_wait(barrier, ns - 1 + nz - 1)

    def row_copy(stream, slot_from, slot_to, r, target):
        return pltpu.make_async_remote_copy(
            src_ref=gp.at[slot_from, r + 1], dst_ref=gp.at[slot_to, r + 1],
            send_sem=z_send.at[stream, r], recv_sem=z_recv.at[slot_to, r],
            device_id={"tm": target}, device_id_type=MESH)

    def to_prev(r):
        return row_copy(TO_PREV, OWN, N1, r, prev)

    def fwd_prev(r):
        return row_copy(FWD_PREV, N1, LATE, r, prev)

    def own_c0(r):
        return row_copy(TO_NEXT, OWN, C0, r, nxt)

    def own_c1(r):
        return row_copy(TO_NEXT, OWN, LATE, r, nxt)

    def fwd_c0(r):
        return row_copy(FWD_C0, C0, C0, r, nxt)

    def cache_copy():
        return pltpu.make_async_remote_copy(
            src_ref=c_ref, dst_ref=cb, send_sem=c_sem.at[0], recv_sem=c_sem.at[1],
            device_id={"tm": prev}, device_id_type=MESH)

    def result_copy(f):
        return pltpu.make_async_remote_copy(
            src_ref=res_out.at[f], dst_ref=res_in.at[f], send_sem=res_sem.at[0, f], recv_sem=res_sem.at[1, f],
            device_id={"tm": nxt}, device_id_type=MESH)

    pl.when(j == last)(lambda: cache_copy().start())
    for i, r in enumerate(order):
        pl.when(j >= 1)(lambda: to_prev(r).start())
        pl.when(j == 0)(lambda: own_c0(r).start())
        if i < 2:
            pl.when(j == 1)(lambda: own_c1(r).start())

    def halo_up(slot):
        return pltpu.make_async_remote_copy(
            src_ref=gp.at[slot, 1], dst_ref=gp.at[slot, rows + 1],
            send_sem=h_send.at[slot, 0], recv_sem=h_recv.at[slot, 0],
            device_id={"space": lax.rem(s + ns - 1, ns)}, device_id_type=MESH)

    def halo_down(slot):
        return pltpu.make_async_remote_copy(
            src_ref=gp.at[slot, rows], dst_ref=gp.at[slot, 0],
            send_sem=h_send.at[slot, 1], recv_sem=h_recv.at[slot, 1],
            device_id={"space": lax.rem(s + 1, ns)}, device_id_type=MESH)

    def halo_start(slot, i):
        pl.when(both(i == 0, s >= 1))(lambda: halo_up(slot).start())
        pl.when(both(i == 1, s < ns - 1))(lambda: halo_down(slot).start())

    for i in range(2):
        halo_start(OWN, jnp.int32(i))

    edge = 2 * channels
    for ref in (xpad, cpad):
        ref[:edge, :] = jnp.zeros((edge, cols), BF16)
        ref[edge + rows * channels:, :] = jnp.zeros((edge, cols), BF16)
    dx[...] = jnp.zeros_like(dx)
    dc[...] = jnp.zeros_like(dc)
    wtx[...] = jnp.zeros_like(wtx)
    wtc[...] = jnp.zeros_like(wtc)
    used = full * width + part
    for tap in range(3):
        flat[tap, used:, :] = jnp.zeros((ns * ck - used, LANES), F32)

    def turn_x(i, carry):
        block = turned(x_ref, i * slab)
        for h in range(rows):
            xpad[pl.ds(pl.multiple_of((h + 2) * channels + i * slab, slab), slab), :] = block[h]
        return carry

    fetch_x.wait()
    lax.fori_loop(0, channels // slab, turn_x, 0)

    def turn_w(i, carry):
        at = pl.multiple_of(lax.rem(i, 3) * channels, slab)
        wlx[lax.div(i, 3), pl.ds(at, channels), :] = w_ref[i].astype(F32).T.astype(BF16)
        return carry

    fetch_w.wait()
    lax.fori_loop(0, 9, turn_w, 0)
    base = jnp.where(j < 2, 0, half)
    for b in range(3):
        at = b * channels
        near = pl.ds(pl.multiple_of(at + base, slab), half)
        wlc[0, at:at + half, :] = wlx[0, near, :]
        wlc[0, at + half:at + channels, :] = wlx[1, near, :]
        wlc[1, at:at + half, :] = jnp.zeros((half, width), BF16)
        wlc[1, at + half:at + channels, :] = wlx[0, near, :]

    def place_cache(lower, upper):
        nothing = jnp.zeros((rows, share, cols), F32)
        for f in range(2):
            low, high = [
                nothing if ref is None else jnp.transpose(ref[f].astype(F32), (1, 0, 2)) for ref in (lower, upper)]
            for h in range(rows):
                at = (h + 2) * channels + f * half
                cpad[at:at + half, :] = jnp.concatenate([low[h], high[h]], axis=0).astype(BF16)

    pl.when(j == 0)(lambda: place_cache(c_ref, None))
    pl.when(j == 1)(lambda: place_cache(None, c_ref))

    lane = lax.broadcasted_iota(jnp.int32, (channels, cols), 1)

    def shift(slot, p, to):
        value = gp[slot, p]
        wide = value.astype(F32)
        sc[to, :channels, :] = jnp.where(lane == cols - 1, 0.0, pltpu.roll(wide, cols - 1, 1)).astype(BF16)
        sc[to, channels:2 * channels, :] = value
        sc[to, 2 * channels:, :] = jnp.where(lane == 0, 0.0, pltpu.roll(wide, 1, 1)).astype(BF16)

    def kernel_sum(wt, pad, index, at, p):
        span = pl.ds(pl.multiple_of(p * channels, slab), width)
        wt[index, :, :width] += lax.dot_general(sc[at], pad[span, :], NT, preferred_element_type=F32)

    def data_sum(wl, out, index, at, p):
        span = pl.ds(pl.multiple_of(p * channels, slab), width)
        out[span, :] += jnp.dot(wl[index], sc[at], preferred_element_type=F32)

    def halo_sums(wt, pad, wl, out, index, at, side):
        h, b = (0, 2) if side == 0 else (rows - 1, 0)
        span = slice((h + 2) * channels, (h + 3) * channels)
        tap = slice(b * channels, (b + 1) * channels)
        wt[index, :, tap] += lax.dot_general(sc[at], pad[span, :], NT, preferred_element_type=F32)
        out[span, :] += jnp.dot(wl[index, tap, :], sc[at], preferred_element_type=F32)

    wide_lane = lax.broadcasted_iota(jnp.int32, (width, wtx.shape[2]), 1)
    in_lower = both(lax.rem(wide_lane, channels) < half, wide_lane < width)
    in_upper = both(lax.rem(wide_lane, channels) >= half, wide_lane < width)
    back = wtx.shape[2] - half

    def pack(tap):
        def put(total):
            for q in range(full):
                flat[tap, q * width:(q + 1) * width, :] = total[:, q * LANES:(q + 1) * LANES]
            tail = total[:, full * LANES:]
            packed = tail[:part]
            for k in range(1, groups):
                packed = packed + pltpu.roll(tail[k * part:(k + 1) * part], k * rem, 1)
            flat[tap, full * width:used, :] = packed

        own = wtx[tap]
        if tap == 2:
            put(own)
            return

        @pl.when(j < 2)
        def _():
            turned_c0 = pltpu.roll(wtc[0], back, 1)
            put(own + jnp.where(
                in_lower, turned_c0 if tap == 1 else wtc[0] + pltpu.roll(wtc[1], back, 1), 0.0))

        @pl.when(j >= 2)
        def _():
            put(own + jnp.where(in_upper, wtc[0] if tap == 1 else pltpu.roll(wtc[0], half, 1) + wtc[1], 0.0))

    def reduction(index):
        def rs_copy(k):
            to = lax.rem(s + k, ns)
            return pltpu.make_async_remote_copy(
                src_ref=sb.at[index, to], dst_ref=rb.at[index, s],
                send_sem=rs_send.at[index, k], recv_sem=rs_recv.at[index, s],
                device_id={"space": to}, device_id_type=MESH)

        def rs_landed(k):
            source = lax.rem(s + ns - k, ns)
            return pltpu.make_async_remote_copy(
                src_ref=sb.at[index, source], dst_ref=rb.at[index, source],
                send_sem=rs_send.at[index, k], recv_sem=rs_recv.at[index, source],
                device_id={"space": source}, device_id_type=MESH)

        def z_copy(k):
            return pltpu.make_async_remote_copy(
                src_ref=zs.at[index], dst_ref=zb.at[index, j],
                send_sem=zz_send.at[index, k], recv_sem=zz_recv.at[index, j],
                device_id={"tm": lax.rem(j + k, nz)}, device_id_type=MESH)

        def z_landed(k):
            source = lax.rem(j + nz - k, nz)
            return pltpu.make_async_remote_copy(
                src_ref=zs.at[index], dst_ref=zb.at[index, source],
                send_sem=zz_send.at[index, k], recv_sem=zz_recv.at[index, source],
                device_id={"tm": source}, device_id_type=MESH)

        def ag_copy(k):
            return pltpu.make_async_remote_copy(
                src_ref=mine.at[index], dst_ref=gb.at[index, s],
                send_sem=ag_send.at[index, k], recv_sem=ag_recv.at[index, s],
                device_id={"space": lax.rem(s + k, ns)}, device_id_type=MESH)

        def ag_landed(k):
            source = lax.rem(s + ns - k, ns)
            return pltpu.make_async_remote_copy(
                src_ref=mine.at[index], dst_ref=gb.at[index, source],
                send_sem=ag_send.at[index, k], recv_sem=ag_recv.at[index, source],
                device_id={"space": source}, device_id_type=MESH)

        def scatter():
            pack(index)
            for q in range(ns):
                sb[index, q] = flat[index, q * ck:(q + 1) * ck, :].astype(BF16)
            for k in range(1, ns):
                rs_copy(k).start()

        def across():
            total = flat[index, pl.ds(pl.multiple_of(s * ck, slab), ck), :]
            for k in range(1, ns):
                rs_landed(k).wait_recv()
                total = total + rb[index, lax.rem(s + ns - k, ns)].astype(F32)
            zs[index] = total.astype(BF16)

        def exchange():
            for k in range(1, nz):
                z_copy(k).start()

        def gather():
            zb[index, j] = zs[index]
            for k in range(1, nz):
                z_landed(k).wait_recv()
            total = zb[index, 0].astype(F32)
            for q in range(1, nz):
                total = total + zb[index, q].astype(F32)
            mine[index] = total.astype(BF16)
            for k in range(1, ns):
                ag_copy(k).start()
            keep().start()

        def keep():
            return pltpu.make_async_copy(mine.at[index], gb.at[index, s], stores.at[index])

        def finish():
            for k in range(1, ns):
                ag_landed(k).wait_recv()
            keep().wait()

        def sent():
            for k in range(1, ns):
                rs_copy(k).wait_send()
                ag_copy(k).wait_send()
            for k in range(1, nz):
                z_copy(k).wait_send()

        return scatter, across, exchange, gather, finish, sent

    steps = [reduction(tap) for tap in range(3)]
    scatter, across, exchange, gather, finish, sent = range(6)

    def middle_row(e):
        r = ordered(e)

        @pl.when(j < last)
        def _():
            row_copy(TO_PREV, OWN, N1, r, prev).wait_recv()
            pl.when(j >= 1)(lambda: fwd_prev(r).start())
            halo_start(N1, e)

        @pl.when(both(j >= 1, j < last))
        def _():
            row_copy(TO_NEXT, OWN, C0, r, nxt).wait_recv()
            pl.when(j == 1)(lambda: fwd_c0(r).start())
            halo_start(C0, e)

        @pl.when(both(j == 1, e == rows - 1))
        def _():
            for q in order[2:]:
                own_c1(q).start()

    def late_row(e):
        @pl.when(j < last)
        def _():
            row_copy(FWD_PREV, N1, LATE, ordered(e), prev).wait_recv()
            halo_start(LATE, e)

    def halo_wait(slot, side):
        if side == 0:
            halo_up(slot).wait_send()
            halo_down(slot).wait_recv()
        else:
            halo_down(slot).wait_send()
            halo_up(slot).wait_recv()

    ahead = jnp.where(j < 2, 1, 0)

    def results(f, offset):
        rows_of = [
            dc[pl.ds(pl.multiple_of((h + 2) * channels + f * half + offset, 8), share), :] for h in range(rows)]
        return jnp.transpose(jnp.stack(rows_of, axis=0).astype(BF16), (1, 0, 2))

    def step(n, carry):
        phase = lax.div(n, rows)
        i = lax.rem(n, rows)
        r = ordered(i)

        @pl.when(both(n >= rows, n + ahead < 2 * rows))
        def _():
            middle_row(n + ahead - rows)

        pl.when(phase == 2)(lambda: late_row(i))

        @pl.when(both(n == rows, j == 2))
        def _():
            cache_copy().wait_recv()
            place_cache(c_ref, cb)

        with_x = jnp.logical_or(phase == 0, jnp.logical_or(both(phase == 1, j < last), j < 2))
        x_slot = phase
        tap = 2 - phase
        with_c = jnp.logical_or(
            both(phase == 0, j < 2), jnp.logical_or(both(phase == 1, j < last), both(phase == 2, j == 2)))
        apart = both(phase >= 1, j >= 1)
        c_slot = jnp.where(apart, jnp.where(phase == 1, C0, LATE), phase)
        c_kind = jnp.where(phase == 0, j, jnp.where(both(phase == 1, j >= 1), 0, 1))
        c_at = jnp.where(apart, 1, 0)

        @pl.when(with_x)
        def _():
            shift(x_slot, r + 1, 0)
            kernel_sum(wtx, xpad, tap, 0, r + 1)
            data_sum(wlx, dx, tap, 0, r + 1)

        @pl.when(with_c)
        def _():
            pl.when(apart)(lambda: shift(c_slot, r + 1, 1))
            kernel_sum(wtc, cpad, c_kind, c_at, r + 1)
            data_sum(wlc, dc, c_kind, c_at, r + 1)

        pl.when(both(n == 2, j < 2))(lambda: middle_row(jnp.int32(0)))

        @pl.when(i == 2)
        def _():
            for side in range(2):
                p = 0 if side == 0 else rows + 1

                @pl.when(s >= 1 if side == 0 else s < ns - 1)
                def _():
                    @pl.when(with_x)
                    def _():
                        halo_wait(x_slot, side)
                        shift(x_slot, p, 0)
                        halo_sums(wtx, xpad, wlx, dx, tap, 0, side)

                    @pl.when(with_c)
                    def _():
                        @pl.when(apart)
                        def _():
                            halo_wait(c_slot, side)
                            shift(c_slot, p, 1)

                        halo_sums(wtc, cpad, wlc, dc, c_kind, c_at, side)

        pl.when(n == rows - 1)(steps[2][scatter])

        @pl.when(n == 2 * rows - 1)
        def _():
            steps[1][scatter]()

            @pl.when(j == 2)
            def _():
                res_out[0] = results(0, share)
                result_copy(0).start()

        return carry

    lax.fori_loop(0, 3 * rows - 1, step, 0)
    steps[2][across]()
    steps[1][across]()

    final = jnp.int32(rows - 1)
    p = order[-1] + 1
    late_row(final)

    @pl.when(j < 2)
    def _():
        shift(LATE, p, 0)
        kernel_sum(wtx, xpad, 0, 0, p)

    @pl.when(j == 2)
    def _():
        shift(LATE, p, 1)
        kernel_sum(wtc, cpad, 1, 1, p)

    steps[0][scatter]()
    steps[2][exchange]()
    steps[1][exchange]()

    @pl.when(j == 2)
    def _():
        data_sum(wlc, dc, 1, 1, p)
        res_out[1] = results(1, share)

    pl.when(j < 2)(lambda: data_sum(wlx, dx, 0, 0, p))

    def turn_out(i, carry):
        block = [
            dx[pl.ds(pl.multiple_of((h + 2) * channels + i * slab, slab), slab), :] for h in range(rows)]
        ig_ref[pl.ds(pl.multiple_of(i * slab, slab), slab)] = jnp.transpose(
            jnp.stack(block, axis=0).astype(BF16), (1, 0, 2))
        return carry

    lax.fori_loop(0, channels // slab, turn_out, 0)
    store_ig = pltpu.make_async_copy(ig_ref, ig_hbm, stores.at[3])
    store_cg = pltpu.make_async_copy(cg_ref, cg_hbm, stores.at[4])
    store_ig.start()

    @pl.when(j < last)
    def _():
        offset = jnp.where(j == 1, share, 0)
        for f in range(2):
            cg_ref[f] = results(f, offset)
        store_cg.start()

    steps[0][across]()
    steps[0][exchange]()
    pl.when(j == 2)(lambda: result_copy(1).start())
    steps[2][gather]()
    steps[1][gather]()
    steps[0][gather]()
    steps[2][finish]()
    steps[1][finish]()

    @pl.when(j == last)
    def _():
        for f in range(2):
            result_copy(f).wait_recv()
            cg_ref[f] = res_in[f]
        store_cg.start()
        cache_copy().wait_send()

    @pl.when(j == 2)
    def _():
        for f in range(2):
            result_copy(f).wait_send()

    for r in range(rows):
        pl.when(j >= 1)(lambda: to_prev(r).wait_send())
        pl.when(both(j >= 1, j < last))(lambda: fwd_prev(r).wait_send())
        pl.when(j == 0)(lambda: own_c0(r).wait_send())

        @pl.when(j == 1)
        def _():
            own_c1(r).wait_send()
            fwd_c0(r).wait_send()

    for tap in range(3):
        steps[tap][sent]()
    store_ig.wait()
    store_cg.wait()
    steps[0][finish]()


def publish(scale, ig_in, cg_in, gb_in, ig_out, cg_out, wg_out, ig, cg, gb, wg, fetches, moves, reads, writes):
    channels = ig_in.shape[0]
    width = wg.shape[2]
    rem = width % LANES
    groups = LANES // rem
    used = (width // LANES) * width + width // groups
    read = [pltpu.make_async_copy(gb_in.at[tap], gb.at[tap], reads.at[tap]) for tap in range(3)]
    for copy in read:
        copy.start()
    cut = channels // (moves.shape[0] - 2)
    parts = [
        (ig_in.at[n * cut:(n + 1) * cut], ig.at[n * cut:(n + 1) * cut], ig_out.at[n * cut:(n + 1) * cut])
        for n in range(moves.shape[0] - 2)]
    parts += [(cg_in.at[f], cg.at[f], cg_out.at[f]) for f in range(2)]
    fetch = [pltpu.make_async_copy(src, held, fetches.at[n]) for n, (src, held, _) in enumerate(parts)]
    move = [pltpu.make_async_copy(held, dst, moves.at[n]) for n, (_, held, dst) in enumerate(parts)]
    for copy in fetch:
        copy.start()
    for copy_in, copy_out in zip(fetch, move):
        copy_in.wait()
        copy_out.start()
    at = lax.broadcasted_iota(jnp.int32, (width, LANES), 1)
    step = LANES - channels
    write = [pltpu.make_async_copy(wg.at[tap], wg_out.at[tap], writes.at[tap]) for tap in range(3)]
    for tap in range(3):
        read[tap].wait()
        first = gb[tap, :width, :].astype(F32) * scale
        second = gb[tap, width:2 * width, :].astype(F32) * scale
        packed = gb[tap, 2 * width:used, :].astype(F32) * scale
        middle = jnp.where(at < step, pltpu.roll(first, step, 1), pltpu.roll(second, step, 1))
        third = jnp.concatenate(
            [pltpu.roll(packed, (2 * step - k * rem) % LANES, 1) if (2 * step - k * rem) % LANES else packed
             for k in range(groups)], axis=0)
        final = jnp.where(at < 2 * step, pltpu.roll(second, 2 * step, 1), third)
        for b, value in enumerate((first, middle, final)):
            wg[tap, b] = value[:, :channels]
        write[tap].start()
    for copy in (*move, *write):
        copy.wait()


def up_to(value, step):
    return -(-value // step) * step


def per_device(nz, ns, frames, cache, grad_out, weight):
    _, channels, rows, cols = frames.shape
    width = 3 * channels
    wide = up_to(width, LANES)
    ck = up_to(-(-(width * channels * 3) // (ns * LANES)), 16)
    scale = 1.0 / math.sqrt(nz * ns * rows * cols)
    hbm = pl.BlockSpec(memory_space=pl.ANY)
    dma = pltpu.SemaphoreType.DMA
    padded = (rows + 4) * channels
    ig, cg, shards = pl.pallas_call(
        functools.partial(kernel, nz, ns, ck),
        out_shape=(
            jax.ShapeDtypeStruct(frames.shape[1:], BF16),
            jax.ShapeDtypeStruct(cache.shape, BF16),
            jax.ShapeDtypeStruct((3, ns, ck, LANES), BF16),
        ),
        in_specs=[hbm] * 4,
        out_specs=(hbm,) * 3,
        scratch_shapes=[
            pltpu.VMEM(frames.shape[1:], BF16),
            pltpu.VMEM(cache.shape, BF16),
            pltpu.VMEM(frames.shape[1:], BF16),
            pltpu.VMEM(frames.shape[1:], BF16),
            pltpu.VMEM(cache.shape, BF16),
            pltpu.VMEM((9, width, channels), BF16),
            pltpu.VMEM((4, rows + 2, channels, cols), BF16),
            pltpu.VMEM((2, width, cols), BF16),
            pltpu.VMEM((padded, cols), BF16), pltpu.VMEM((padded, cols), BF16),
            pltpu.VMEM((padded, cols), F32), pltpu.VMEM((padded, cols), F32),
            pltpu.VMEM((3, width, width), BF16), pltpu.VMEM((2, width, width), BF16),
            pltpu.VMEM((3, width, wide), F32), pltpu.VMEM((2, width, wide), F32),
            pltpu.VMEM((3, ns * ck, LANES), F32),
            pltpu.VMEM((3, ns, ck, LANES), BF16), pltpu.VMEM((3, ns, ck, LANES), BF16),
            pltpu.VMEM((3, ck, LANES), BF16), pltpu.VMEM((3, nz, ck, LANES), BF16),
            pltpu.VMEM((3, ck, LANES), BF16),
            pltpu.VMEM(cache.shape, BF16), pltpu.VMEM(cache.shape, BF16), pltpu.VMEM(cache.shape, BF16),
            dma((4,)),
            dma((4, rows)), dma((4, rows)), dma((4, 2)), dma((4, 2)),
            dma((3, ns)), dma((3, ns)), dma((3, nz)), dma((3, nz)), dma((3, ns)), dma((3, ns)),
            dma((2,)), dma((2, 2)), dma((5,)),
        ],
        compiler_params=pltpu.CompilerParams(
            collective_id=0, has_side_effects=True, vmem_limit_bytes=60 * 1024 * 1024),
    )(grad_out[0], frames[0], cache, weight.reshape(9, width, channels))
    ig, cg, weight_grad = pl.pallas_call(
        functools.partial(publish, scale),
        out_shape=(
            jax.ShapeDtypeStruct(frames.shape[1:], BF16),
            jax.ShapeDtypeStruct(cache.shape, BF16),
            jax.ShapeDtypeStruct((3, 3, width, channels), F32),
        ),
        in_specs=[hbm] * 3,
        out_specs=(hbm,) * 3,
        scratch_shapes=[
            pltpu.VMEM(frames.shape[1:], BF16), pltpu.VMEM(cache.shape, BF16),
            pltpu.VMEM((3, ns * ck, LANES), BF16), pltpu.VMEM((3, 3, width, channels), F32),
            dma((6,)), dma((6,)), dma((3,)), dma((3,)),
        ],
        compiler_params=pltpu.CompilerParams(vmem_limit_bytes=60 * 1024 * 1024),
    )(ig, cg, shards.reshape(3, ns * ck, LANES))
    return ig[None], cg, weight_grad.reshape(weight.shape)


def solution(mesh):
    placed = (
        P("tm", None, "space", None),
        P(None, "tm", "space", None),
        P("tm", None, "space", None),
        P(),
    )
    return jax.shard_map(
        functools.partial(per_device, mesh.shape["tm"], mesh.shape["space"]),
        mesh=mesh,
        in_specs=placed,
        out_specs=(P("tm", None, "space", None), P(None, "tm", "space", None), P()),
        check_vma=False,
    )
```

```python
import functools
import math

import jax
import jax.numpy as jnp
from jax import lax
from jax.experimental import pallas as pl
from jax.experimental.pallas import tpu as pltpu
from jax.sharding import PartitionSpec as P

MESH = pl.DeviceIdType.MESH
OWN, N1, LATE, C0 = range(4)
TO_PREV, FWD_PREV, TO_NEXT, FWD_C0 = range(4)
NT = (((1,), (1,)), ((), ()))
LANES = 128
F32, BF16 = jnp.float32, jnp.bfloat16


def kernel(
    nz, ns, ck,
    g_hbm, x_hbm, c_hbm, w_hbm, ig_hbm, cg_hbm, gb,
    ig_ref, cg_ref, g_ref, x_ref, c_ref, w_ref,
    gp, sc, xpad, cpad, dx, dc, wlx, wlc, wtx, wtc, flat,
    sb, rb, zs, zb, mine, cb, res_out, res_in,
    loads, z_send, z_recv, h_send, h_recv,
    rs_send, rs_recv, zz_send, zz_recv, ag_send, ag_recv, c_sem, res_sem, stores,
):
    assert nz == 4
    j = lax.axis_index("tm")
    s = lax.axis_index("space")
    channels, rows, cols = g_ref.shape
    share = c_ref.shape[1]
    half = 2 * share
    assert channels == 2 * half and rows >= 4
    width = 3 * channels
    full, rem = width // LANES, width % LANES
    groups = LANES // rem
    part = width // groups
    assert full == 2 and LANES % rem == 0 and part % 8 == 0
    last = nz - 1
    order = [0, rows - 1, *range(1, rows - 1)]
    slab = 16
    prev = lax.rem(j + nz - 1, nz)
    nxt = lax.rem(j + 1, nz)

    def both(*terms):
        return functools.reduce(jnp.logical_and, terms)

    def ordered(i):
        return jnp.where(i == 0, 0, jnp.where(i == 1, rows - 1, i - 1))

    fetch_g, fetch_c, fetch_x, fetch_w = [
        pltpu.make_async_copy(src, dst, loads.at[n])
        for n, (src, dst) in enumerate(((g_hbm, g_ref), (c_hbm, c_ref), (x_hbm, x_ref), (w_hbm, w_ref)))]
    for copy in (fetch_g, fetch_c, fetch_x, fetch_w):
        copy.start()
    barrier = pltpu.get_barrier_semaphore()
    for k in range(1, ns):
        pl.semaphore_signal(barrier, inc=1, device_id={"space": lax.rem(s + k, ns)}, device_id_type=MESH)
    for k in range(1, nz):
        pl.semaphore_signal(barrier, inc=1, device_id={"tm": lax.rem(j + k, nz)}, device_id_type=MESH)

    def turned(ref, at):
        return jnp.transpose(ref[pl.ds(pl.multiple_of(at, slab), slab)], (1, 0, 2))

    def turn_g(i, carry):
        gp[OWN, 1:rows + 1, pl.ds(pl.multiple_of(i * slab, slab), slab), :] = turned(g_ref, i * slab)
        return carry

    fetch_g.wait()
    lax.fori_loop(0, channels // slab, turn_g, 0)
    fetch_c.wait()
    pl.semaphore_wait(barrier, ns - 1 + nz - 1)

    def row_copy(stream, slot_from, slot_to, r, target):
        return pltpu.make_async_remote_copy(
            src_ref=gp.at[slot_from, r + 1], dst_ref=gp.at[slot_to, r + 1],
            send_sem=z_send.at[stream, r], recv_sem=z_recv.at[slot_to, r],
            device_id={"tm": target}, device_id_type=MESH)

    def to_prev(r):
        return row_copy(TO_PREV, OWN, N1, r, prev)

    def fwd_prev(r):
        return row_copy(FWD_PREV, N1, LATE, r, prev)

    def own_c0(r):
        return row_copy(TO_NEXT, OWN, C0, r, nxt)

    def own_c1(r):
        return row_copy(TO_NEXT, OWN, LATE, r, nxt)

    def fwd_c0(r):
        return row_copy(FWD_C0, C0, C0, r, nxt)

    def cache_copy():
        return pltpu.make_async_remote_copy(
            src_ref=c_ref, dst_ref=cb, send_sem=c_sem.at[0], recv_sem=c_sem.at[1],
            device_id={"tm": prev}, device_id_type=MESH)

    def result_copy(f):
        return pltpu.make_async_remote_copy(
            src_ref=res_out.at[f], dst_ref=res_in.at[f], send_sem=res_sem.at[0, f], recv_sem=res_sem.at[1, f],
            device_id={"tm": nxt}, device_id_type=MESH)

    pl.when(j == last)(lambda: cache_copy().start())
    for i, r in enumerate(order):
        pl.when(j >= 1)(lambda: to_prev(r).start())
        pl.when(j == 0)(lambda: own_c0(r).start())
        if i < 2:
            pl.when(j == 1)(lambda: own_c1(r).start())

    def halo_up(slot):
        return pltpu.make_async_remote_copy(
            src_ref=gp.at[slot, 1], dst_ref=gp.at[slot, rows + 1],
            send_sem=h_send.at[slot, 0], recv_sem=h_recv.at[slot, 0],
            device_id={"space": lax.rem(s + ns - 1, ns)}, device_id_type=MESH)

    def halo_down(slot):
        return pltpu.make_async_remote_copy(
            src_ref=gp.at[slot, rows], dst_ref=gp.at[slot, 0],
            send_sem=h_send.at[slot, 1], recv_sem=h_recv.at[slot, 1],
            device_id={"space": lax.rem(s + 1, ns)}, device_id_type=MESH)

    def halo_start(slot, i):
        pl.when(both(i == 0, s >= 1))(lambda: halo_up(slot).start())
        pl.when(both(i == 1, s < ns - 1))(lambda: halo_down(slot).start())

    for i in range(2):
        halo_start(OWN, jnp.int32(i))

    edge = 2 * channels
    for ref in (xpad, cpad):
        ref[:edge, :] = jnp.zeros((edge, cols), BF16)
        ref[edge + rows * channels:, :] = jnp.zeros((edge, cols), BF16)
    dx[...] = jnp.zeros_like(dx)
    dc[...] = jnp.zeros_like(dc)
    wtx[...] = jnp.zeros_like(wtx)
    wtc[...] = jnp.zeros_like(wtc)
    used = full * width + part
    for tap in range(3):
        flat[tap, used:, :] = jnp.zeros((ns * ck - used, LANES), F32)

    def turn_x(i, carry):
        block = turned(x_ref, i * slab)
        for h in range(rows):
            xpad[pl.ds(pl.multiple_of((h + 2) * channels + i * slab, slab), slab), :] = block[h]
        return carry

    fetch_x.wait()
    lax.fori_loop(0, channels // slab, turn_x, 0)

    def turn_w(i, carry):
        at = pl.multiple_of(lax.rem(i, 3) * channels, slab)
        wlx[lax.div(i, 3), pl.ds(at, channels), :] = w_ref[i].astype(F32).T.astype(BF16)
        return carry

    fetch_w.wait()
    lax.fori_loop(0, 9, turn_w, 0)
    base = jnp.where(j < 2, 0, half)
    for b in range(3):
        at = b * channels
        near = pl.ds(pl.multiple_of(at + base, slab), half)
        wlc[0, at:at + half, :] = wlx[0, near, :]
        wlc[0, at + half:at + channels, :] = wlx[1, near, :]
        wlc[1, at:at + half, :] = jnp.zeros((half, width), BF16)
        wlc[1, at + half:at + channels, :] = wlx[0, near, :]

    def place_cache(lower, upper):
        nothing = jnp.zeros((rows, share, cols), F32)
        for f in range(2):
            low, high = [
                nothing if ref is None else jnp.transpose(ref[f].astype(F32), (1, 0, 2)) for ref in (lower, upper)]
            for h in range(rows):
                at = (h + 2) * channels + f * half
                cpad[at:at + half, :] = jnp.concatenate([low[h], high[h]], axis=0).astype(BF16)

    pl.when(j == 0)(lambda: place_cache(c_ref, None))
    pl.when(j == 1)(lambda: place_cache(None, c_ref))

    lane = lax.broadcasted_iota(jnp.int32, (channels, cols), 1)

    def shift(slot, p, to):
        value = gp[slot, p]
        wide = value.astype(F32)
        sc[to, :channels, :] = jnp.where(lane == cols - 1, 0.0, pltpu.roll(wide, cols - 1, 1)).astype(BF16)
        sc[to, channels:2 * channels, :] = value
        sc[to, 2 * channels:, :] = jnp.where(lane == 0, 0.0, pltpu.roll(wide, 1, 1)).astype(BF16)

    def kernel_sum(wt, pad, index, at, p):
        span = pl.ds(pl.multiple_of(p * channels, slab), width)
        wt[index, :, :width] += lax.dot_general(sc[at], pad[span, :], NT, preferred_element_type=F32)

    def data_sum(wl, out, index, at, p):
        span = pl.ds(pl.multiple_of(p * channels, slab), width)
        out[span, :] += jnp.dot(wl[index], sc[at], preferred_element_type=F32)

    def halo_sums(wt, pad, wl, out, index, at, side):
        h, b = (0, 2) if side == 0 else (rows - 1, 0)
        span = slice((h + 2) * channels, (h + 3) * channels)
        tap = slice(b * channels, (b + 1) * channels)
        wt[index, :, tap] += lax.dot_general(sc[at], pad[span, :], NT, preferred_element_type=F32)
        out[span, :] += jnp.dot(wl[index, tap, :], sc[at], preferred_element_type=F32)

    wide_lane = lax.broadcasted_iota(jnp.int32, (width, wtx.shape[2]), 1)
    in_lower = both(lax.rem(wide_lane, channels) < half, wide_lane < width)
    in_upper = both(lax.rem(wide_lane, channels) >= half, wide_lane < width)
    back = wtx.shape[2] - half

    def pack(tap):
        def put(total):
            for q in range(full):
                flat[tap, q * width:(q + 1) * width, :] = total[:, q * LANES:(q + 1) * LANES]
            tail = total[:, full * LANES:]
            packed = tail[:part]
            for k in range(1, groups):
                packed = packed + pltpu.roll(tail[k * part:(k + 1) * part], k * rem, 1)
            flat[tap, full * width:used, :] = packed

        own = wtx[tap]
        if tap == 2:
            put(own)
            return

        @pl.when(j < 2)
        def _():
            turned_c0 = pltpu.roll(wtc[0], back, 1)
            put(own + jnp.where(
                in_lower, turned_c0 if tap == 1 else wtc[0] + pltpu.roll(wtc[1], back, 1), 0.0))

        @pl.when(j >= 2)
        def _():
            put(own + jnp.where(in_upper, wtc[0] if tap == 1 else pltpu.roll(wtc[0], half, 1) + wtc[1], 0.0))

    def reduction(index):
        def rs_copy(k):
            to = lax.rem(s + k, ns)
            return pltpu.make_async_remote_copy(
                src_ref=sb.at[index, to], dst_ref=rb.at[index, s],
                send_sem=rs_send.at[index, k], recv_sem=rs_recv.at[index, s],
                device_id={"space": to}, device_id_type=MESH)

        def rs_landed(k):
            source = lax.rem(s + ns - k, ns)
            return pltpu.make_async_remote_copy(
                src_ref=sb.at[index, source], dst_ref=rb.at[index, source],
                send_sem=rs_send.at[index, k], recv_sem=rs_recv.at[index, source],
                device_id={"space": source}, device_id_type=MESH)

        def z_copy(k):
            return pltpu.make_async_remote_copy(
                src_ref=zs.at[index], dst_ref=zb.at[index, j],
                send_sem=zz_send.at[index, k], recv_sem=zz_recv.at[index, j],
                device_id={"tm": lax.rem(j + k, nz)}, device_id_type=MESH)

        def z_landed(k):
            source = lax.rem(j + nz - k, nz)
            return pltpu.make_async_remote_copy(
                src_ref=zs.at[index], dst_ref=zb.at[index, source],
                send_sem=zz_send.at[index, k], recv_sem=zz_recv.at[index, source],
                device_id={"tm": source}, device_id_type=MESH)

        def ag_copy(k):
            return pltpu.make_async_remote_copy(
                src_ref=mine.at[index], dst_ref=gb.at[index, s],
                send_sem=ag_send.at[index, k], recv_sem=ag_recv.at[index, s],
                device_id={"space": lax.rem(s + k, ns)}, device_id_type=MESH)

        def ag_landed(k):
            source = lax.rem(s + ns - k, ns)
            return pltpu.make_async_remote_copy(
                src_ref=mine.at[index], dst_ref=gb.at[index, source],
                send_sem=ag_send.at[index, k], recv_sem=ag_recv.at[index, source],
                device_id={"space": source}, device_id_type=MESH)

        def scatter():
            pack(index)
            for q in range(ns):
                sb[index, q] = flat[index, q * ck:(q + 1) * ck, :].astype(BF16)
            for k in range(1, ns):
                rs_copy(k).start()

        def across():
            total = flat[index, pl.ds(pl.multiple_of(s * ck, slab), ck), :]
            for k in range(1, ns):
                rs_landed(k).wait_recv()
                total = total + rb[index, lax.rem(s + ns - k, ns)].astype(F32)
            zs[index] = total.astype(BF16)

        holders = nz if index == 2 else last

        def exchange():
            @pl.when(j < holders)
            def _():
                for k in range(1, nz):
                    z_copy(k).start()

        def gather():
            pl.when(j < holders)(lambda: zb.__setitem__((index, j), zs[index]))
            for k in range(1, nz):
                pl.when(lax.rem(j + nz - k, nz) < holders)(lambda: z_landed(k).wait_recv())
            total = zb[index, 0].astype(F32)
            for q in range(1, holders):
                total = total + zb[index, q].astype(F32)
            mine[index] = total.astype(BF16)
            for k in range(1, ns):
                ag_copy(k).start()
            keep().start()

        def keep():
            return pltpu.make_async_copy(mine.at[index], gb.at[index, s], stores.at[index])

        def finish():
            for k in range(1, ns):
                ag_landed(k).wait_recv()
            keep().wait()

        def sent():
            for k in range(1, ns):
                rs_copy(k).wait_send()
                ag_copy(k).wait_send()
            @pl.when(j < holders)
            def _():
                for k in range(1, nz):
                    z_copy(k).wait_send()

        return scatter, across, exchange, gather, finish, sent

    steps = [reduction(tap) for tap in range(3)]
    scatter, across, exchange, gather, finish, sent = range(6)

    def middle_row(e):
        r = ordered(e)

        @pl.when(j < last)
        def _():
            row_copy(TO_PREV, OWN, N1, r, prev).wait_recv()
            pl.when(j >= 1)(lambda: fwd_prev(r).start())
            halo_start(N1, e)

        @pl.when(both(j >= 1, j < last))
        def _():
            row_copy(TO_NEXT, OWN, C0, r, nxt).wait_recv()
            pl.when(j == 1)(lambda: fwd_c0(r).start())
            halo_start(C0, e)

        @pl.when(both(j == 1, e == rows - 1))
        def _():
            for q in order[2:]:
                own_c1(q).start()

    def late_row(e):
        @pl.when(j < last)
        def _():
            row_copy(FWD_PREV, N1, LATE, ordered(e), prev).wait_recv()
            halo_start(LATE, e)

    def halo_wait(slot, side):
        if side == 0:
            halo_up(slot).wait_send()
            halo_down(slot).wait_recv()
        else:
            halo_down(slot).wait_send()
            halo_up(slot).wait_recv()

    ahead = jnp.where(j < 2, 1, 0)

    def results(f, offset):
        rows_of = [
            dc[pl.ds(pl.multiple_of((h + 2) * channels + f * half + offset, 8), share), :] for h in range(rows)]
        return jnp.transpose(jnp.stack(rows_of, axis=0).astype(BF16), (1, 0, 2))

    def step(n, carry):
        phase = lax.div(n, rows)
        i = lax.rem(n, rows)
        r = ordered(i)

        @pl.when(both(n >= rows, n + ahead < 2 * rows))
        def _():
            middle_row(n + ahead - rows)

        pl.when(phase == 2)(lambda: late_row(i))

        @pl.when(both(n == rows, j == 2))
        def _():
            cache_copy().wait_recv()
            place_cache(c_ref, cb)

        with_x = jnp.logical_or(phase == 0, jnp.logical_or(both(phase == 1, j < last), j < 2))
        x_slot = phase
        tap = 2 - phase
        with_c = jnp.logical_or(
            both(phase == 0, j < 2), jnp.logical_or(both(phase == 1, j < last), both(phase == 2, j == 2)))
        apart = both(phase >= 1, j >= 1)
        c_slot = jnp.where(apart, jnp.where(phase == 1, C0, LATE), phase)
        c_kind = jnp.where(phase == 0, j, jnp.where(both(phase == 1, j >= 1), 0, 1))
        c_at = jnp.where(apart, 1, 0)

        @pl.when(with_x)
        def _():
            shift(x_slot, r + 1, 0)
            kernel_sum(wtx, xpad, tap, 0, r + 1)
            data_sum(wlx, dx, tap, 0, r + 1)

        @pl.when(with_c)
        def _():
            pl.when(apart)(lambda: shift(c_slot, r + 1, 1))
            kernel_sum(wtc, cpad, c_kind, c_at, r + 1)
            data_sum(wlc, dc, c_kind, c_at, r + 1)

        pl.when(both(n == 2, j < 2))(lambda: middle_row(jnp.int32(0)))

        @pl.when(i == 2)
        def _():
            for side in range(2):
                p = 0 if side == 0 else rows + 1

                @pl.when(s >= 1 if side == 0 else s < ns - 1)
                def _():
                    @pl.when(with_x)
                    def _():
                        halo_wait(x_slot, side)
                        shift(x_slot, p, 0)
                        halo_sums(wtx, xpad, wlx, dx, tap, 0, side)

                    @pl.when(with_c)
                    def _():
                        @pl.when(apart)
                        def _():
                            halo_wait(c_slot, side)
                            shift(c_slot, p, 1)

                        halo_sums(wtc, cpad, wlc, dc, c_kind, c_at, side)

        pl.when(n == rows - 1)(steps[2][scatter])

        @pl.when(n == 2 * rows - 1)
        def _():
            steps[1][scatter]()

            @pl.when(j == 2)
            def _():
                res_out[0] = results(0, share)
                result_copy(0).start()

        return carry

    lax.fori_loop(0, 3 * rows - 1, step, 0)
    steps[2][across]()
    steps[1][across]()

    final = jnp.int32(rows - 1)
    p = order[-1] + 1
    late_row(final)
    steps[2][exchange]()
    steps[1][exchange]()

    @pl.when(j < 2)
    def _():
        shift(LATE, p, 0)
        kernel_sum(wtx, xpad, 0, 0, p)

    @pl.when(j == 2)
    def _():
        shift(LATE, p, 1)
        kernel_sum(wtc, cpad, 1, 1, p)

    steps[0][scatter]()

    @pl.when(j == 2)
    def _():
        data_sum(wlc, dc, 1, 1, p)
        res_out[1] = results(1, share)

    pl.when(j < 2)(lambda: data_sum(wlx, dx, 0, 0, p))

    def turn_out(i, carry):
        block = [
            dx[pl.ds(pl.multiple_of((h + 2) * channels + i * slab, slab), slab), :] for h in range(rows)]
        ig_ref[pl.ds(pl.multiple_of(i * slab, slab), slab)] = jnp.transpose(
            jnp.stack(block, axis=0).astype(BF16), (1, 0, 2))
        return carry

    lax.fori_loop(0, channels // slab, turn_out, 0)
    store_ig = pltpu.make_async_copy(ig_ref, ig_hbm, stores.at[3])
    store_cg = pltpu.make_async_copy(cg_ref, cg_hbm, stores.at[4])
    store_ig.start()

    @pl.when(j < last)
    def _():
        offset = jnp.where(j == 1, share, 0)
        for f in range(2):
            cg_ref[f] = results(f, offset)
        store_cg.start()

    steps[0][across]()
    steps[0][exchange]()
    pl.when(j == 2)(lambda: result_copy(1).start())
    steps[2][gather]()
    steps[1][gather]()
    steps[0][gather]()
    steps[2][finish]()
    steps[1][finish]()

    @pl.when(j == last)
    def _():
        for f in range(2):
            result_copy(f).wait_recv()
            cg_ref[f] = res_in[f]
        store_cg.start()
        cache_copy().wait_send()

    @pl.when(j == 2)
    def _():
        for f in range(2):
            result_copy(f).wait_send()

    for r in range(rows):
        pl.when(j >= 1)(lambda: to_prev(r).wait_send())
        pl.when(both(j >= 1, j < last))(lambda: fwd_prev(r).wait_send())
        pl.when(j == 0)(lambda: own_c0(r).wait_send())

        @pl.when(j == 1)
        def _():
            own_c1(r).wait_send()
            fwd_c0(r).wait_send()

    for tap in range(3):
        steps[tap][sent]()
    store_ig.wait()
    store_cg.wait()
    steps[0][finish]()


def publish(scale, ig_in, cg_in, gb_in, ig_out, cg_out, wg_out, ig, cg, gb, wg, fetches, moves, reads, writes):
    channels = ig_in.shape[0]
    width = wg.shape[2]
    rem = width % LANES
    groups = LANES // rem
    used = (width // LANES) * width + width // groups
    read = [pltpu.make_async_copy(gb_in.at[tap], gb.at[tap], reads.at[tap]) for tap in range(3)]
    for copy in read:
        copy.start()
    cut = channels // (moves.shape[0] - 2)
    parts = [
        (ig_in.at[n * cut:(n + 1) * cut], ig.at[n * cut:(n + 1) * cut], ig_out.at[n * cut:(n + 1) * cut])
        for n in range(moves.shape[0] - 2)]
    parts += [(cg_in.at[f], cg.at[f], cg_out.at[f]) for f in range(2)]
    fetch = [pltpu.make_async_copy(src, held, fetches.at[n]) for n, (src, held, _) in enumerate(parts)]
    move = [pltpu.make_async_copy(held, dst, moves.at[n]) for n, (_, held, dst) in enumerate(parts)]
    for copy in fetch:
        copy.start()
    for copy_in, copy_out in zip(fetch, move):
        copy_in.wait()
        copy_out.start()
    at = lax.broadcasted_iota(jnp.int32, (width, LANES), 1)
    step = LANES - channels
    write = [pltpu.make_async_copy(wg.at[tap], wg_out.at[tap], writes.at[tap]) for tap in range(3)]
    for tap in range(3):
        read[tap].wait()
        first = gb[tap, :width, :].astype(F32) * scale
        second = gb[tap, width:2 * width, :].astype(F32) * scale
        packed = gb[tap, 2 * width:used, :].astype(F32) * scale
        middle = jnp.where(at < step, pltpu.roll(first, step, 1), pltpu.roll(second, step, 1))
        third = jnp.concatenate(
            [pltpu.roll(packed, (2 * step - k * rem) % LANES, 1) if (2 * step - k * rem) % LANES else packed
             for k in range(groups)], axis=0)
        final = jnp.where(at < 2 * step, pltpu.roll(second, 2 * step, 1), third)
        for b, value in enumerate((first, middle, final)):
            wg[tap, b] = value[:, :channels]
        write[tap].start()
    for copy in (*move, *write):
        copy.wait()


def up_to(value, step):
    return -(-value // step) * step


def per_device(nz, ns, frames, cache, grad_out, weight):
    _, channels, rows, cols = frames.shape
    width = 3 * channels
    wide = up_to(width, LANES)
    ck = up_to(-(-(width * channels * 3) // (ns * LANES)), 16)
    scale = 1.0 / math.sqrt(nz * ns * rows * cols)
    hbm = pl.BlockSpec(memory_space=pl.ANY)
    dma = pltpu.SemaphoreType.DMA
    padded = (rows + 4) * channels
    ig, cg, shards = pl.pallas_call(
        functools.partial(kernel, nz, ns, ck),
        out_shape=(
            jax.ShapeDtypeStruct(frames.shape[1:], BF16),
            jax.ShapeDtypeStruct(cache.shape, BF16),
            jax.ShapeDtypeStruct((3, ns, ck, LANES), BF16),
        ),
        in_specs=[hbm] * 4,
        out_specs=(hbm,) * 3,
        scratch_shapes=[
            pltpu.VMEM(frames.shape[1:], BF16),
            pltpu.VMEM(cache.shape, BF16),
            pltpu.VMEM(frames.shape[1:], BF16),
            pltpu.VMEM(frames.shape[1:], BF16),
            pltpu.VMEM(cache.shape, BF16),
            pltpu.VMEM((9, width, channels), BF16),
            pltpu.VMEM((4, rows + 2, channels, cols), BF16),
            pltpu.VMEM((2, width, cols), BF16),
            pltpu.VMEM((padded, cols), BF16), pltpu.VMEM((padded, cols), BF16),
            pltpu.VMEM((padded, cols), F32), pltpu.VMEM((padded, cols), F32),
            pltpu.VMEM((3, width, width), BF16), pltpu.VMEM((2, width, width), BF16),
            pltpu.VMEM((3, width, wide), F32), pltpu.VMEM((2, width, wide), F32),
            pltpu.VMEM((3, ns * ck, LANES), F32),
            pltpu.VMEM((3, ns, ck, LANES), BF16), pltpu.VMEM((3, ns, ck, LANES), BF16),
            pltpu.VMEM((3, ck, LANES), BF16), pltpu.VMEM((3, nz, ck, LANES), BF16),
            pltpu.VMEM((3, ck, LANES), BF16),
            pltpu.VMEM(cache.shape, BF16), pltpu.VMEM(cache.shape, BF16), pltpu.VMEM(cache.shape, BF16),
            dma((4,)),
            dma((4, rows)), dma((4, rows)), dma((4, 2)), dma((4, 2)),
            dma((3, ns)), dma((3, ns)), dma((3, nz)), dma((3, nz)), dma((3, ns)), dma((3, ns)),
            dma((2,)), dma((2, 2)), dma((5,)),
        ],
        compiler_params=pltpu.CompilerParams(
            collective_id=0, has_side_effects=True, vmem_limit_bytes=60 * 1024 * 1024),
    )(grad_out[0], frames[0], cache, weight.reshape(9, width, channels))
    ig, cg, weight_grad = pl.pallas_call(
        functools.partial(publish, scale),
        out_shape=(
            jax.ShapeDtypeStruct(frames.shape[1:], BF16),
            jax.ShapeDtypeStruct(cache.shape, BF16),
            jax.ShapeDtypeStruct((3, 3, width, channels), F32),
        ),
        in_specs=[hbm] * 3,
        out_specs=(hbm,) * 3,
        scratch_shapes=[
            pltpu.VMEM(frames.shape[1:], BF16), pltpu.VMEM(cache.shape, BF16),
            pltpu.VMEM((3, ns * ck, LANES), BF16), pltpu.VMEM((3, 3, width, channels), F32),
            dma((6,)), dma((6,)), dma((3,)), dma((3,)),
        ],
        compiler_params=pltpu.CompilerParams(vmem_limit_bytes=60 * 1024 * 1024),
    )(ig, cg, shards.reshape(3, ns * ck, LANES))
    return ig[None], cg, weight_grad.reshape(weight.shape)


def solution(mesh):
    placed = (
        P("tm", None, "space", None),
        P(None, "tm", "space", None),
        P("tm", None, "space", None),
        P(),
    )
    return jax.shard_map(
        functools.partial(per_device, mesh.shape["tm"], mesh.shape["space"]),
        mesh=mesh,
        in_specs=placed,
        out_specs=(P("tm", None, "space", None), P(None, "tm", "space", None), P()),
        check_vma=False,
    )
```

```python
import functools
import math

import jax
import jax.numpy as jnp
from jax import lax
from jax.experimental import pallas as pl
from jax.experimental.pallas import tpu as pltpu
from jax.sharding import PartitionSpec as P

MESH = pl.DeviceIdType.MESH
OWN, N1, LATE, C0 = range(4)
TO_PREV, FWD_PREV, TO_NEXT, FWD_C0 = range(4)
NT = (((1,), (1,)), ((), ()))
LANES = 128
F32, BF16 = jnp.float32, jnp.bfloat16


def kernel(
    nz, ns, ck,
    g_hbm, x_hbm, c_hbm, w_hbm, ig_hbm, cg_hbm, gb,
    ig_ref, cg_ref, g_ref, x_ref, c_ref, w_ref,
    gp, sc, xpad, cpad, dx, dc, wlx, wlc, wtx, wtc, flat,
    sb, rb, zs, zb, mine, cb, res_out, res_in,
    loads, z_send, z_recv, h_send, h_recv,
    rs_send, rs_recv, zz_send, zz_recv, ag_send, ag_recv, c_sem, res_sem, stores,
):
    assert nz == 4
    j = lax.axis_index("tm")
    s = lax.axis_index("space")
    channels, rows, cols = g_ref.shape
    share = c_ref.shape[1]
    half = 2 * share
    assert channels == 2 * half and rows >= 4
    width = 3 * channels
    full, rem = width // LANES, width % LANES
    groups = LANES // rem
    part = width // groups
    assert full == 2 and LANES % rem == 0 and part % 8 == 0
    last = nz - 1
    order = [0, rows - 1, *range(1, rows - 1)]
    slab = 16
    prev = lax.rem(j + nz - 1, nz)
    nxt = lax.rem(j + 1, nz)

    def both(*terms):
        return functools.reduce(jnp.logical_and, terms)

    def ordered(i):
        return jnp.where(i == 0, 0, jnp.where(i == 1, rows - 1, i - 1))

    fetch_g, fetch_c, fetch_x, fetch_w = [
        pltpu.make_async_copy(src, dst, loads.at[n])
        for n, (src, dst) in enumerate(((g_hbm, g_ref), (c_hbm, c_ref), (x_hbm, x_ref), (w_hbm, w_ref)))]
    for copy in (fetch_g, fetch_c, fetch_x, fetch_w):
        copy.start()
    barrier = pltpu.get_barrier_semaphore()
    for k in range(1, ns):
        pl.semaphore_signal(barrier, inc=1, device_id={"space": lax.rem(s + k, ns)}, device_id_type=MESH)
    for k in range(1, nz):
        pl.semaphore_signal(barrier, inc=1, device_id={"tm": lax.rem(j + k, nz)}, device_id_type=MESH)

    def turned(ref, at):
        return jnp.transpose(ref[pl.ds(pl.multiple_of(at, slab), slab)], (1, 0, 2))

    def turn_g(i, carry):
        gp[OWN, 1:rows + 1, pl.ds(pl.multiple_of(i * slab, slab), slab), :] = turned(g_ref, i * slab)
        return carry

    fetch_g.wait()
    lax.fori_loop(0, channels // slab, turn_g, 0)
    fetch_c.wait()
    pl.semaphore_wait(barrier, ns - 1 + nz - 1)

    def row_copy(stream, slot_from, slot_to, r, target):
        return pltpu.make_async_remote_copy(
            src_ref=gp.at[slot_from, r + 1], dst_ref=gp.at[slot_to, r + 1],
            send_sem=z_send.at[stream, r], recv_sem=z_recv.at[slot_to, r],
            device_id={"tm": target}, device_id_type=MESH)

    def to_prev(r):
        return row_copy(TO_PREV, OWN, N1, r, prev)

    def fwd_prev(r):
        return row_copy(FWD_PREV, N1, LATE, r, prev)

    def own_c0(r):
        return row_copy(TO_NEXT, OWN, C0, r, nxt)

    def own_c1(r):
        return row_copy(TO_NEXT, OWN, LATE, r, nxt)

    def fwd_c0(r):
        return row_copy(FWD_C0, C0, C0, r, nxt)

    def cache_copy():
        return pltpu.make_async_remote_copy(
            src_ref=c_ref, dst_ref=cb, send_sem=c_sem.at[0], recv_sem=c_sem.at[1],
            device_id={"tm": prev}, device_id_type=MESH)

    def result_copy(f):
        return pltpu.make_async_remote_copy(
            src_ref=res_out.at[f], dst_ref=res_in.at[f], send_sem=res_sem.at[0, f], recv_sem=res_sem.at[1, f],
            device_id={"tm": nxt}, device_id_type=MESH)

    pl.when(j == last)(lambda: cache_copy().start())
    for i, r in enumerate(order):
        pl.when(j >= 1)(lambda: to_prev(r).start())
        pl.when(j == 0)(lambda: own_c0(r).start())
        if i < 2:
            pl.when(j == 1)(lambda: own_c1(r).start())

    def halo_up(slot):
        return pltpu.make_async_remote_copy(
            src_ref=gp.at[slot, 1], dst_ref=gp.at[slot, rows + 1],
            send_sem=h_send.at[slot, 0], recv_sem=h_recv.at[slot, 0],
            device_id={"space": lax.rem(s + ns - 1, ns)}, device_id_type=MESH)

    def halo_down(slot):
        return pltpu.make_async_remote_copy(
            src_ref=gp.at[slot, rows], dst_ref=gp.at[slot, 0],
            send_sem=h_send.at[slot, 1], recv_sem=h_recv.at[slot, 1],
            device_id={"space": lax.rem(s + 1, ns)}, device_id_type=MESH)

    def halo_start(slot, i):
        pl.when(both(i == 0, s >= 1))(lambda: halo_up(slot).start())
        pl.when(both(i == 1, s < ns - 1))(lambda: halo_down(slot).start())

    for i in range(2):
        halo_start(OWN, jnp.int32(i))

    edge = 2 * channels
    for ref in (xpad, cpad):
        ref[:edge, :] = jnp.zeros((edge, cols), BF16)
        ref[edge + rows * channels:, :] = jnp.zeros((edge, cols), BF16)
    dx[...] = jnp.zeros_like(dx)
    dc[...] = jnp.zeros_like(dc)
    wtx[...] = jnp.zeros_like(wtx)
    wtc[...] = jnp.zeros_like(wtc)
    used = full * width + part
    for tap in range(3):
        flat[tap, used:, :] = jnp.zeros((ns * ck - used, LANES), F32)

    def turn_x(i, carry):
        block = turned(x_ref, i * slab)
        for h in range(rows):
            xpad[pl.ds(pl.multiple_of((h + 2) * channels + i * slab, slab), slab), :] = block[h]
        return carry

    fetch_x.wait()
    lax.fori_loop(0, channels // slab, turn_x, 0)

    def turn_w(i, carry):
        at = pl.multiple_of(lax.rem(i, 3) * channels, slab)
        wlx[lax.div(i, 3), pl.ds(at, channels), :] = w_ref[i].astype(F32).T.astype(BF16)
        return carry

    fetch_w.wait()
    lax.fori_loop(0, 9, turn_w, 0)
    base = jnp.where(j < 2, 0, half)
    for b in range(3):
        at = b * channels
        near = pl.ds(pl.multiple_of(at + base, slab), half)
        wlc[0, at:at + half, :] = wlx[0, near, :]
        wlc[0, at + half:at + channels, :] = wlx[1, near, :]
        wlc[1, at:at + half, :] = jnp.zeros((half, width), BF16)
        wlc[1, at + half:at + channels, :] = wlx[0, near, :]

    def place_cache(lower, upper):
        nothing = jnp.zeros((rows, share, cols), F32)
        for f in range(2):
            low, high = [
                nothing if ref is None else jnp.transpose(ref[f].astype(F32), (1, 0, 2)) for ref in (lower, upper)]
            for h in range(rows):
                at = (h + 2) * channels + f * half
                cpad[at:at + half, :] = jnp.concatenate([low[h], high[h]], axis=0).astype(BF16)

    pl.when(j == 0)(lambda: place_cache(c_ref, None))
    pl.when(j == 1)(lambda: place_cache(None, c_ref))

    lane = lax.broadcasted_iota(jnp.int32, (channels, cols), 1)

    def shift(slot, p, to):
        value = gp[slot, p]
        wide = value.astype(F32)
        sc[to, :channels, :] = jnp.where(lane == cols - 1, 0.0, pltpu.roll(wide, cols - 1, 1)).astype(BF16)
        sc[to, channels:2 * channels, :] = value
        sc[to, 2 * channels:, :] = jnp.where(lane == 0, 0.0, pltpu.roll(wide, 1, 1)).astype(BF16)

    def kernel_sum(wt, pad, index, at, p):
        span = pl.ds(pl.multiple_of(p * channels, slab), width)
        wt[index, :, :width] += lax.dot_general(sc[at], pad[span, :], NT, preferred_element_type=F32)

    def data_sum(wl, out, index, at, p):
        span = pl.ds(pl.multiple_of(p * channels, slab), width)
        out[span, :] += jnp.dot(wl[index], sc[at], preferred_element_type=F32)

    def halo_sums(wt, pad, wl, out, index, at, side):
        h, b = (0, 2) if side == 0 else (rows - 1, 0)
        span = slice((h + 2) * channels, (h + 3) * channels)
        tap = slice(b * channels, (b + 1) * channels)
        wt[index, :, tap] += lax.dot_general(sc[at], pad[span, :], NT, preferred_element_type=F32)
        out[span, :] += jnp.dot(wl[index, tap, :], sc[at], preferred_element_type=F32)

    wide_lane = lax.broadcasted_iota(jnp.int32, (width, wtx.shape[2]), 1)
    in_lower = both(lax.rem(wide_lane, channels) < half, wide_lane < width)
    in_upper = both(lax.rem(wide_lane, channels) >= half, wide_lane < width)
    back = wtx.shape[2] - half

    def pack(tap):
        def put(total):
            for q in range(full):
                flat[tap, q * width:(q + 1) * width, :] = total[:, q * LANES:(q + 1) * LANES]
            tail = total[:, full * LANES:]
            packed = tail[:part]
            for k in range(1, groups):
                packed = packed + pltpu.roll(tail[k * part:(k + 1) * part], k * rem, 1)
            flat[tap, full * width:used, :] = packed

        own = wtx[tap]
        if tap == 2:
            put(own)
            return

        @pl.when(j < 2)
        def _():
            turned_c0 = pltpu.roll(wtc[0], back, 1)
            put(own + jnp.where(
                in_lower, turned_c0 if tap == 1 else wtc[0] + pltpu.roll(wtc[1], back, 1), 0.0))

        @pl.when(j >= 2)
        def _():
            put(own + jnp.where(in_upper, wtc[0] if tap == 1 else pltpu.roll(wtc[0], half, 1) + wtc[1], 0.0))

    def reduction(index):
        def rs_copy(k):
            to = lax.rem(s + k, ns)
            return pltpu.make_async_remote_copy(
                src_ref=sb.at[index, to], dst_ref=rb.at[index, s],
                send_sem=rs_send.at[index, k], recv_sem=rs_recv.at[index, s],
                device_id={"space": to}, device_id_type=MESH)

        def rs_landed(k):
            source = lax.rem(s + ns - k, ns)
            return pltpu.make_async_remote_copy(
                src_ref=sb.at[index, source], dst_ref=rb.at[index, source],
                send_sem=rs_send.at[index, k], recv_sem=rs_recv.at[index, source],
                device_id={"space": source}, device_id_type=MESH)

        def z_copy(k):
            return pltpu.make_async_remote_copy(
                src_ref=zs.at[index], dst_ref=zb.at[index, j],
                send_sem=zz_send.at[index, k], recv_sem=zz_recv.at[index, j],
                device_id={"tm": lax.rem(j + k, nz)}, device_id_type=MESH)

        def z_landed(k):
            source = lax.rem(j + nz - k, nz)
            return pltpu.make_async_remote_copy(
                src_ref=zs.at[index], dst_ref=zb.at[index, source],
                send_sem=zz_send.at[index, k], recv_sem=zz_recv.at[index, source],
                device_id={"tm": source}, device_id_type=MESH)

        def ag_copy(k):
            return pltpu.make_async_remote_copy(
                src_ref=mine.at[index], dst_ref=gb.at[index, s],
                send_sem=ag_send.at[index, k], recv_sem=ag_recv.at[index, s],
                device_id={"space": lax.rem(s + k, ns)}, device_id_type=MESH)

        def ag_landed(k):
            source = lax.rem(s + ns - k, ns)
            return pltpu.make_async_remote_copy(
                src_ref=mine.at[index], dst_ref=gb.at[index, source],
                send_sem=ag_send.at[index, k], recv_sem=ag_recv.at[index, source],
                device_id={"space": source}, device_id_type=MESH)

        def scatter():
            pack(index)
            for q in range(ns):
                sb[index, q] = flat[index, q * ck:(q + 1) * ck, :].astype(BF16)
            for k in sorted(range(1, ns), key=lambda k: abs(k - ns // 2)):
                rs_copy(k).start()

        def across():
            total = flat[index, pl.ds(pl.multiple_of(s * ck, slab), ck), :]
            for k in range(1, ns):
                rs_landed(k).wait_recv()
                total = total + rb[index, lax.rem(s + ns - k, ns)].astype(F32)
            zs[index] = total.astype(BF16)

        holders = nz if index == 2 else last

        def exchange():
            @pl.when(j < holders)
            def _():
                for k in range(1, nz):
                    z_copy(k).start()

        def gather():
            pl.when(j < holders)(lambda: zb.__setitem__((index, j), zs[index]))
            for k in range(1, nz):
                pl.when(lax.rem(j + nz - k, nz) < holders)(lambda: z_landed(k).wait_recv())
            total = zb[index, 0].astype(F32)
            for q in range(1, holders):
                total = total + zb[index, q].astype(F32)
            mine[index] = total.astype(BF16)
            for k in sorted(range(1, ns), key=lambda k: abs(k - ns // 2)):
                ag_copy(k).start()
            keep().start()

        def keep():
            return pltpu.make_async_copy(mine.at[index], gb.at[index, s], stores.at[index])

        def finish():
            for k in range(1, ns):
                ag_landed(k).wait_recv()
            keep().wait()

        def sent():
            for k in range(1, ns):
                rs_copy(k).wait_send()
            if index:
                return
            for k in range(1, ns):
                ag_copy(k).wait_send()

            @pl.when(j < holders)
            def _():
                for k in range(1, nz):
                    z_copy(k).wait_send()

        return scatter, across, exchange, gather, finish, sent, z_copy, z_landed

    steps = [reduction(tap) for tap in range(3)]
    scatter, across, exchange, gather, finish, sent, z_copy, z_landed = range(8)

    early = pl.ds(1, 2)

    def pair_z(source, to, k):
        return pltpu.make_async_remote_copy(
            src_ref=zs.at[early], dst_ref=zb.at[early, source],
            send_sem=zz_send.at[1, k], recv_sem=zz_recv.at[1, source],
            device_id={"tm": to}, device_id_type=MESH)

    def pair_ag(source, to, k):
        return pltpu.make_async_remote_copy(
            src_ref=mine.at[early], dst_ref=gb.at[early, source],
            send_sem=ag_send.at[1, k], recv_sem=ag_recv.at[1, source],
            device_id={"space": to}, device_id_type=MESH)

    def pair_keep():
        return pltpu.make_async_copy(mine.at[early], gb.at[early, s], stores.at[1])

    def pair_exchange():
        for k in range(1, nz):
            pl.when(j < last)(lambda: pair_z(j, lax.rem(j + k, nz), k).start())
            pl.when(j == last)(lambda: steps[2][z_copy](k).start())

    def pair_gather():
        zb[2, j] = zs[2]

        @pl.when(j < last)
        def _():
            zb[1, j] = zs[1]

        for k in range(1, nz):
            source = lax.rem(j + nz - k, nz)
            pl.when(source < last)(lambda: pair_z(source, source, k).wait_recv())
            pl.when(source == last)(lambda: steps[2][z_landed](k).wait_recv())
        for tap, holders in ((2, nz), (1, last)):
            total = zb[tap, 0].astype(F32)
            for q in range(1, holders):
                total = total + zb[tap, q].astype(F32)
            mine[tap] = total.astype(BF16)
        for k in sorted(range(1, ns), key=lambda k: abs(k - ns // 2)):
            pair_ag(s, lax.rem(s + k, ns), k).start()
        pair_keep().start()

    def pair_finish():
        for k in range(1, ns):
            source = lax.rem(s + ns - k, ns)
            pair_ag(source, source, k).wait_recv()
        pair_keep().wait()

    def pair_sent():
        for k in range(1, ns):
            pair_ag(s, lax.rem(s + k, ns), k).wait_send()
        for k in range(1, nz):
            pl.when(j < last)(lambda: pair_z(j, lax.rem(j + k, nz), k).wait_send())
            pl.when(j == last)(lambda: steps[2][z_copy](k).wait_send())

    def middle_row(e):
        r = ordered(e)

        @pl.when(j < last)
        def _():
            row_copy(TO_PREV, OWN, N1, r, prev).wait_recv()
            pl.when(j >= 1)(lambda: fwd_prev(r).start())
            halo_start(N1, e)

        @pl.when(both(j >= 1, j < last))
        def _():
            row_copy(TO_NEXT, OWN, C0, r, nxt).wait_recv()
            pl.when(j == 1)(lambda: fwd_c0(r).start())
            halo_start(C0, e)

        @pl.when(both(j == 1, e == rows - 1))
        def _():
            for q in order[2:]:
                own_c1(q).start()

    def late_row(e):
        @pl.when(j < last)
        def _():
            row_copy(FWD_PREV, N1, LATE, ordered(e), prev).wait_recv()
            halo_start(LATE, e)

    def halo_wait(slot, side):
        if side == 0:
            halo_up(slot).wait_send()
            halo_down(slot).wait_recv()
        else:
            halo_down(slot).wait_send()
            halo_up(slot).wait_recv()

    ahead = jnp.where(j < 2, 1, 0)

    def results(f, offset):
        rows_of = [
            dc[pl.ds(pl.multiple_of((h + 2) * channels + f * half + offset, 8), share), :] for h in range(rows)]
        return jnp.transpose(jnp.stack(rows_of, axis=0).astype(BF16), (1, 0, 2))

    def step(n, carry):
        phase = lax.div(n, rows)
        i = lax.rem(n, rows)
        r = ordered(i)

        @pl.when(both(n >= rows, n + ahead < 2 * rows))
        def _():
            middle_row(n + ahead - rows)

        pl.when(phase == 2)(lambda: late_row(i))

        @pl.when(both(n == rows, j == 2))
        def _():
            cache_copy().wait_recv()
            place_cache(c_ref, cb)

        with_x = jnp.logical_or(phase == 0, jnp.logical_or(both(phase == 1, j < last), j < 2))
        x_slot = phase
        tap = 2 - phase
        with_c = jnp.logical_or(
            both(phase == 0, j < 2), jnp.logical_or(both(phase == 1, j < last), both(phase == 2, j == 2)))
        apart = both(phase >= 1, j >= 1)
        c_slot = jnp.where(apart, jnp.where(phase == 1, C0, LATE), phase)
        c_kind = jnp.where(phase == 0, j, jnp.where(both(phase == 1, j >= 1), 0, 1))
        c_at = jnp.where(apart, 1, 0)

        @pl.when(with_x)
        def _():
            shift(x_slot, r + 1, 0)
            kernel_sum(wtx, xpad, tap, 0, r + 1)
            data_sum(wlx, dx, tap, 0, r + 1)

        @pl.when(with_c)
        def _():
            pl.when(apart)(lambda: shift(c_slot, r + 1, 1))
            kernel_sum(wtc, cpad, c_kind, c_at, r + 1)
            data_sum(wlc, dc, c_kind, c_at, r + 1)

        pl.when(both(n == 2, j < 2))(lambda: middle_row(jnp.int32(0)))

        @pl.when(i == 2)
        def _():
            for side in range(2):
                p = 0 if side == 0 else rows + 1

                @pl.when(s >= 1 if side == 0 else s < ns - 1)
                def _():
                    @pl.when(with_x)
                    def _():
                        halo_wait(x_slot, side)
                        shift(x_slot, p, 0)
                        halo_sums(wtx, xpad, wlx, dx, tap, 0, side)

                    @pl.when(with_c)
                    def _():
                        @pl.when(apart)
                        def _():
                            halo_wait(c_slot, side)
                            shift(c_slot, p, 1)

                        halo_sums(wtc, cpad, wlc, dc, c_kind, c_at, side)

        pl.when(n == rows - 1)(steps[2][scatter])

        @pl.when(n == 2 * rows - 1)
        def _():
            steps[1][scatter]()

            @pl.when(j == 2)
            def _():
                res_out[0] = results(0, share)
                result_copy(0).start()

        return carry

    lax.fori_loop(0, 3 * rows - 1, step, 0)
    steps[2][across]()
    steps[1][across]()

    final = jnp.int32(rows - 1)
    p = order[-1] + 1
    late_row(final)
    pair_exchange()

    @pl.when(j < 2)
    def _():
        shift(LATE, p, 0)
        kernel_sum(wtx, xpad, 0, 0, p)

    @pl.when(j == 2)
    def _():
        shift(LATE, p, 1)
        kernel_sum(wtc, cpad, 1, 1, p)

    steps[0][scatter]()

    @pl.when(j == 2)
    def _():
        data_sum(wlc, dc, 1, 1, p)
        res_out[1] = results(1, share)

    pl.when(j < 2)(lambda: data_sum(wlx, dx, 0, 0, p))

    def turn_out(i, carry):
        block = [
            dx[pl.ds(pl.multiple_of((h + 2) * channels + i * slab, slab), slab), :] for h in range(rows)]
        ig_ref[pl.ds(pl.multiple_of(i * slab, slab), slab)] = jnp.transpose(
            jnp.stack(block, axis=0).astype(BF16), (1, 0, 2))
        return carry

    lax.fori_loop(0, channels // slab, turn_out, 0)
    store_ig = pltpu.make_async_copy(ig_ref, ig_hbm, stores.at[3])
    store_cg = pltpu.make_async_copy(cg_ref, cg_hbm, stores.at[4])
    store_ig.start()

    @pl.when(j < last)
    def _():
        offset = jnp.where(j == 1, share, 0)
        for f in range(2):
            cg_ref[f] = results(f, offset)
        store_cg.start()

    steps[0][across]()
    steps[0][exchange]()
    pl.when(j == 2)(lambda: result_copy(1).start())
    pair_gather()
    steps[0][gather]()
    pair_finish()

    @pl.when(j == last)
    def _():
        for f in range(2):
            result_copy(f).wait_recv()
            cg_ref[f] = res_in[f]
        store_cg.start()
        cache_copy().wait_send()

    @pl.when(j == 2)
    def _():
        for f in range(2):
            result_copy(f).wait_send()

    for r in range(rows):
        pl.when(j >= 1)(lambda: to_prev(r).wait_send())
        pl.when(both(j >= 1, j < last))(lambda: fwd_prev(r).wait_send())
        pl.when(j == 0)(lambda: own_c0(r).wait_send())

        @pl.when(j == 1)
        def _():
            own_c1(r).wait_send()
            fwd_c0(r).wait_send()

    for tap in range(3):
        steps[tap][sent]()
    pair_sent()
    store_ig.wait()
    store_cg.wait()
    steps[0][finish]()


def publish(scale, ig_in, cg_in, gb_in, ig_out, cg_out, wg_out, ig, cg, gb, wg, fetches, moves, reads, writes):
    channels = ig_in.shape[0]
    width = wg.shape[2]
    rem = width % LANES
    groups = LANES // rem
    used = (width // LANES) * width + width // groups
    read = [pltpu.make_async_copy(gb_in.at[tap], gb.at[tap], reads.at[tap]) for tap in range(3)]
    for copy in read:
        copy.start()
    cut = channels // (moves.shape[0] - 2)
    parts = [
        (ig_in.at[n * cut:(n + 1) * cut], ig.at[n * cut:(n + 1) * cut], ig_out.at[n * cut:(n + 1) * cut])
        for n in range(moves.shape[0] - 2)]
    parts += [(cg_in.at[f], cg.at[f], cg_out.at[f]) for f in range(2)]
    fetch = [pltpu.make_async_copy(src, held, fetches.at[n]) for n, (src, held, _) in enumerate(parts)]
    move = [pltpu.make_async_copy(held, dst, moves.at[n]) for n, (_, held, dst) in enumerate(parts)]
    for copy in fetch:
        copy.start()
    for copy_in, copy_out in zip(fetch, move):
        copy_in.wait()
        copy_out.start()
    at = lax.broadcasted_iota(jnp.int32, (width, LANES), 1)
    step = LANES - channels
    write = [pltpu.make_async_copy(wg.at[tap], wg_out.at[tap], writes.at[tap]) for tap in range(3)]
    for tap in range(3):
        read[tap].wait()
        first = gb[tap, :width, :].astype(F32) * scale
        second = gb[tap, width:2 * width, :].astype(F32) * scale
        packed = gb[tap, 2 * width:used, :].astype(F32) * scale
        middle = jnp.where(at < step, pltpu.roll(first, step, 1), pltpu.roll(second, step, 1))
        third = jnp.concatenate(
            [pltpu.roll(packed, (2 * step - k * rem) % LANES, 1) if (2 * step - k * rem) % LANES else packed
             for k in range(groups)], axis=0)
        final = jnp.where(at < 2 * step, pltpu.roll(second, 2 * step, 1), third)
        for b, value in enumerate((first, middle, final)):
            wg[tap, b] = value[:, :channels]
        write[tap].start()
    for copy in (*move, *write):
        copy.wait()


def up_to(value, step):
    return -(-value // step) * step


def per_device(nz, ns, frames, cache, grad_out, weight):
    _, channels, rows, cols = frames.shape
    width = 3 * channels
    wide = up_to(width, LANES)
    ck = up_to(-(-(width * channels * 3) // (ns * LANES)), 16)
    scale = 1.0 / math.sqrt(nz * ns * rows * cols)
    hbm = pl.BlockSpec(memory_space=pl.ANY)
    dma = pltpu.SemaphoreType.DMA
    padded = (rows + 4) * channels
    ig, cg, shards = pl.pallas_call(
        functools.partial(kernel, nz, ns, ck),
        out_shape=(
            jax.ShapeDtypeStruct(frames.shape[1:], BF16),
            jax.ShapeDtypeStruct(cache.shape, BF16),
            jax.ShapeDtypeStruct((3, ns, ck, LANES), BF16),
        ),
        in_specs=[hbm] * 4,
        out_specs=(hbm,) * 3,
        scratch_shapes=[
            pltpu.VMEM(frames.shape[1:], BF16),
            pltpu.VMEM(cache.shape, BF16),
            pltpu.VMEM(frames.shape[1:], BF16),
            pltpu.VMEM(frames.shape[1:], BF16),
            pltpu.VMEM(cache.shape, BF16),
            pltpu.VMEM((9, width, channels), BF16),
            pltpu.VMEM((4, rows + 2, channels, cols), BF16),
            pltpu.VMEM((2, width, cols), BF16),
            pltpu.VMEM((padded, cols), BF16), pltpu.VMEM((padded, cols), BF16),
            pltpu.VMEM((padded, cols), F32), pltpu.VMEM((padded, cols), F32),
            pltpu.VMEM((3, width, width), BF16), pltpu.VMEM((2, width, width), BF16),
            pltpu.VMEM((3, width, wide), F32), pltpu.VMEM((2, width, wide), F32),
            pltpu.VMEM((3, ns * ck, LANES), F32),
            pltpu.VMEM((3, ns, ck, LANES), BF16), pltpu.VMEM((3, ns, ck, LANES), BF16),
            pltpu.VMEM((3, ck, LANES), BF16), pltpu.VMEM((3, nz, ck, LANES), BF16),
            pltpu.VMEM((3, ck, LANES), BF16),
            pltpu.VMEM(cache.shape, BF16), pltpu.VMEM(cache.shape, BF16), pltpu.VMEM(cache.shape, BF16),
            dma((4,)),
            dma((4, rows)), dma((4, rows)), dma((4, 2)), dma((4, 2)),
            dma((3, ns)), dma((3, ns)), dma((3, nz)), dma((3, nz)), dma((3, ns)), dma((3, ns)),
            dma((2,)), dma((2, 2)), dma((5,)),
        ],
        compiler_params=pltpu.CompilerParams(
            collective_id=0, has_side_effects=True, vmem_limit_bytes=60 * 1024 * 1024),
    )(grad_out[0], frames[0], cache, weight.reshape(9, width, channels))
    ig, cg, weight_grad = pl.pallas_call(
        functools.partial(publish, scale),
        out_shape=(
            jax.ShapeDtypeStruct(frames.shape[1:], BF16),
            jax.ShapeDtypeStruct(cache.shape, BF16),
            jax.ShapeDtypeStruct((3, 3, width, channels), F32),
        ),
        in_specs=[hbm] * 3,
        out_specs=(hbm,) * 3,
        scratch_shapes=[
            pltpu.VMEM(frames.shape[1:], BF16), pltpu.VMEM(cache.shape, BF16),
            pltpu.VMEM((3, ns * ck, LANES), BF16), pltpu.VMEM((3, 3, width, channels), F32),
            dma((3,)), dma((3,)), dma((3,)), dma((3,)),
        ],
        compiler_params=pltpu.CompilerParams(vmem_limit_bytes=60 * 1024 * 1024),
    )(ig, cg, shards.reshape(3, ns * ck, LANES))
    return ig[None], cg, weight_grad.reshape(weight.shape)


def solution(mesh):
    placed = (
        P("tm", None, "space", None),
        P(None, "tm", "space", None),
        P("tm", None, "space", None),
        P(),
    )
    return jax.shard_map(
        functools.partial(per_device, mesh.shape["tm"], mesh.shape["space"]),
        mesh=mesh,
        in_specs=placed,
        out_specs=(P("tm", None, "space", None), P(None, "tm", "space", None), P()),
        check_vma=False,
    )
```
